32 devices in a mesh: news: 2 (over x), entity: 16 (over z, y, core).
Axes of the slice: x: 2, y: 2, z: 4, core: 2. Of those that a mesh axis runs over, the one named last changes fastest.
Arguments:
- companies: bfloat16 [16384, 512], P('entity'), may hold values from -200 to 200
- queries: bfloat16 [256, 512], P(('news', 'entity')), may hold values from -2600 to 2600
Outputs:
- pooled: float32 [256, 512], P(('news', 'entity'))
The draws below stay inside these ranges and needn't reach their ends.
All inputs are finite; a program needn't handle non-finite values.
Results may differ from the reference program's by a relative error of at most 0.0076.
Values may be sent and summed in bfloat16 or wider, within the bound.
A program may use at most 64 MiB of HBM per device.

```python
import math
import jax
import jax.numpy as jnp
from jax import lax

D = 512
R_DEV = 1024
ITERS = 3
ROWS = 16384
QB = 128
NQ = 256
N_NEWS = 2


def slab_parts(key):
    column_order = jax.random.permutation(jax.random.fold_in(key, 108), D).astype(jnp.int32)
    spread = (column_order.astype(jnp.float32) + jax.random.uniform(jax.random.fold_in(key, 101), (D,), jnp.float32)) / D
    columns = jnp.exp(spread * math.log(10.0))
    low_half = (column_order < D // 2).astype(jnp.float32)
    group_count = D // 16
    group_index = jnp.minimum(column_order // 8, group_count - 1)
    group_factors = jnp.clip(jax.random.normal(jax.random.fold_in(key, 109), (ROWS, group_count), jnp.float32), -3.0, 3.0)
    group_part = jnp.take(group_factors, group_index, axis=1)
    block_count = ROWS // R_DEV
    loadings = jnp.clip(jax.random.normal(jax.random.fold_in(key, 110), (block_count, D), jnp.float32), -2.0, 2.0)
    sector = jnp.clip(jax.random.normal(jax.random.fold_in(key, 111), (ROWS,), jnp.float32), -3.0, 3.0)
    block_part = sector[:, None] * jnp.repeat(loadings, R_DEV, axis=0)
    structure = low_half[None, :] * (1.2 * group_part + 0.8 * block_part)
    row_scales = 0.5 * jnp.exp(jax.random.uniform(jax.random.fold_in(key, 102), (ROWS,), jnp.float32) * math.log(10.0))
    noise = jnp.clip(jax.random.normal(jax.random.fold_in(key, 103), (ROWS, D), jnp.float32), -4.0, 4.0)
    slab_values = (noise + structure) * columns[None, :] * row_scales[:, None]
    return (slab_values, columns)


def draw_companies(key, part):
    slab_values, columns = slab_parts(key)
    return slab_values.astype(jnp.bfloat16)


def draw_queries(key, part):
    slab_values, columns = slab_parts(key)
    query_scales = 0.5 * jnp.exp(jax.random.uniform(jax.random.fold_in(key, 107), (NQ,), jnp.float32) * math.log(4.0))
    noise = jnp.clip(jax.random.normal(jax.random.fold_in(key, 106), (NQ, D), jnp.float32), -4.0, 4.0)
    query_values = noise * columns[None, :] * query_scales[:, None]
    return query_values.astype(jnp.bfloat16)


def setup_inputs(seed: int = 0) -> dict:
    seeds = jax.random.split(jax.random.key(seed), 3)
    return {
        "companies": draw_companies(jax.random.fold_in(seeds[2], 71), 0),
        "queries": draw_queries(jax.random.fold_in(seeds[2], 71), 0),
    }


RIDGE = 0.05
EPSILON = 1e-06

def product(first_mat, second_mat):
    return jnp.dot(first_mat, second_mat, precision=lax.Precision.HIGHEST, preferred_element_type=jnp.float32)

def inverse_root(gram_full):
    identity = jnp.eye(D, dtype=jnp.float32)
    frob_norm = jnp.sqrt(jnp.sum(gram_full * gram_full) + EPSILON)
    y_iter = gram_full / frob_norm
    z_iter = identity
    for sweep_idx in range(ITERS):
        t_iter = 0.5 * (3.0 * identity - product(z_iter, y_iter))
        y_iter = product(y_iter, t_iter)
        z_iter = product(z_iter, t_iter)
    return (z_iter / jnp.sqrt(frob_norm)).astype(jnp.bfloat16)

def reference(companies, queries):
    gram_full = jnp.dot(companies.T, companies, preferred_element_type=jnp.float32) / ROWS
    gram_full = gram_full + RIDGE * jnp.eye(D, dtype=jnp.float32)
    whitener = inverse_root(gram_full)
    white_slab = jnp.dot(companies, whitener, preferred_element_type=jnp.float32).astype(jnp.bfloat16)
    white_query = jnp.dot(queries, whitener, preferred_element_type=jnp.float32).astype(jnp.bfloat16)
    score_scale = D ** (-0.5)

    def pool_block(query_block):
        scores = jnp.dot(query_block, white_slab.T, preferred_element_type=jnp.float32) * score_scale
        row_top = lax.optimization_barrier(jnp.max(scores, axis=1, keepdims=True))
        weights = jnp.exp(scores - row_top)
        denom = lax.optimization_barrier(jnp.sum(weights, axis=1))
        summed = jnp.dot(weights.astype(jnp.bfloat16), white_slab, preferred_element_type=jnp.float32)
        return summed / denom[:, None]
    pooled = lax.map(pool_block, white_query.reshape(N_NEWS, QB, D))
    return pooled.reshape(NQ, D)
```

```python
import functools

import jax
import jax.numpy as jnp
from jax import lax
from jax.experimental import pallas as pl
from jax.experimental.pallas import tpu as pltpu
from jax.sharding import PartitionSpec as P

RIDGE = 0.05
EPSILON = 1e-06
MESH = pl.DeviceIdType.MESH
LANES = 128
TILE = 16
F32 = jnp.float32
BF16 = jnp.bfloat16


def dot(first_mat, second_mat):
    return jnp.dot(first_mat, second_mat, preferred_element_type=F32)


def product(first_mat, second_mat):
    return dot(first_mat.astype(BF16), second_mat.astype(BF16))


def three_parts(value):
    high = value.astype(BF16).astype(F32)
    middle = (value - high).astype(BF16).astype(F32)
    return [high, middle, value - high - middle]


def remote(src_ref, dst_ref, sems, number, peer):
    send_sem, recv_sem = sems
    return pltpu.make_async_remote_copy(
        src_ref=src_ref,
        dst_ref=dst_ref,
        send_sem=send_sem.at[number],
        recv_sem=recv_sem.at[number],
        device_id={"entity": peer},
        device_id_type=MESH,
    )


def wait_bytes(ref, sem):
    pltpu.make_async_copy(ref, ref, sem).wait()


def kernel(
    n_entity,
    comp_hbm,
    query_hbm,
    out_ref,
    comp,
    query_all,
    query_f32,
    gram_send,
    gram_pair,
    gram_recv,
    gram_all,
    gram,
    part_send,
    part_recv,
    load_sem,
    send_sem,
    recv_sem,
):
    rows, width = comp.shape
    count = query_hbm.shape[0]
    total_rows = rows * n_entity
    n_blocks = width // LANES
    per_piece = gram_send.shape[1]
    me = lax.axis_index("entity")
    half = n_entity // 2
    chip, core = me // 2, lax.rem(me, 2)
    sibling = me + 1 - 2 * core
    my_slot = core * half + chip
    sems = (send_sem, recv_sem)

    load = pltpu.make_async_copy(comp_hbm, comp, load_sem.at[0])
    load.start()
    load_query = pltpu.make_async_copy(query_hbm, query_all.at[my_slot], load_sem.at[1])
    load_query.start()
    barrier = pltpu.get_barrier_semaphore()
    peers = [(hop, lax.rem(chip + hop, half)) for hop in range(1, half)]
    others = [(hop, lax.rem(me + hop, n_entity)) for hop in range(1, n_entity)]
    for _, partner in others:
        pl.semaphore_signal(
            barrier, inc=1, device_id={"entity": partner}, device_id_type=MESH
        )
    load.wait()

    blocks = [(i, j) for i in range(n_blocks) for j in range(i, n_blocks)]
    per_block = LANES // TILE
    partial = {}
    for i in range(n_blocks):
        row_part = lax.dot_general(
            comp[:, i * LANES : (i + 1) * LANES],
            comp[:, i * LANES :],
            (((0,), (0,)), ((), ())),
            preferred_element_type=F32,
        )
        row_part = row_part / total_rows
        for j in range(i, n_blocks):
            number = blocks.index((i, j))
            for t in range(per_block):
                piece, slot = divmod(number * per_block + t, per_piece)
                gram_send[piece, slot] = row_part[
                    t * TILE : (t + 1) * TILE, (j - i) * LANES : (j - i + 1) * LANES
                ].astype(BF16)
    for t in range(len(blocks) * per_block, n_entity * per_piece):
        piece, slot = divmod(t, per_piece)
        gram_send[piece, slot] = jnp.zeros((TILE, LANES), BF16)

    load_query.wait()
    pl.semaphore_wait(barrier, n_entity - 1)

    own_half = pl.ds(core * half, half)
    other_half = pl.ds((1 - core) * half, half)
    to_pair = remote(gram_send.at[other_half], gram_pair, sems, 0, sibling)
    to_pair.start()
    for hop, there in peers:
        remote(query_all.at[my_slot], query_all.at[my_slot], sems, 2, 2 * there + core).start()
    to_pair.wait_recv()
    for k in range(half):
        gram_pair[k] = (gram_pair[k].astype(F32) + gram_send[core * half + k].astype(F32)).astype(
            gram_pair.dtype
        )
    for hop, there in peers:
        remote(gram_pair.at[there], gram_recv.at[hop - 1], sems, 1, 2 * there + core).start()
    total = gram_pair[chip].astype(F32)
    wait_bytes(gram_recv, recv_sem.at[1])
    for k in range(half - 1):
        total = total + gram_recv[k].astype(F32)
    gram_all[my_slot] = total.astype(gram_all.dtype)
    for hop, there in peers:
        remote(gram_all.at[my_slot], gram_all.at[my_slot], sems, 3, 2 * there + core).start()
    wait_bytes(query_all.at[pl.ds(0, half - 1)], recv_sem.at[2])
    query_forward = remote(query_all.at[own_half], query_all.at[own_half], sems, 5, sibling)
    query_forward.start()
    wait_bytes(gram_all.at[pl.ds(0, half - 1)], recv_sem.at[3])
    gram_forward = remote(gram_all.at[own_half], gram_all.at[own_half], sems, 4, sibling)
    gram_forward.start()

    def unpack(first_tile, last_tile):
        for number, (i, j) in enumerate(blocks):
            for t in range(per_block):
                tile = number * per_block + t
                if first_tile <= tile < last_tile:
                    piece, slot = divmod(tile, per_piece)
                    gram[
                        i * LANES + t * TILE : i * LANES + (t + 1) * TILE,
                        j * LANES : (j + 1) * LANES,
                    ] = gram_all[piece, slot].astype(F32)

    middle, last = half * per_piece, n_entity * per_piece
    pl.when(core == 0)(lambda: unpack(0, middle))
    pl.when(core == 1)(lambda: unpack(middle, last))
    gram_forward.wait_recv()
    pl.when(core == 0)(lambda: unpack(middle, last))
    pl.when(core == 1)(lambda: unpack(0, middle))
    for i, j in blocks:
        if i != j:
            gram[j * LANES : (j + 1) * LANES, i * LANES : (i + 1) * LANES] = gram[
                i * LANES : (i + 1) * LANES, j * LANES : (j + 1) * LANES
            ].T

    row_ids = lax.broadcasted_iota(jnp.int32, (width, width), 0)
    col_ids = lax.broadcasted_iota(jnp.int32, (width, width), 1)
    identity = (row_ids == col_ids).astype(F32)
    full = gram[...] + RIDGE * identity
    squares = jnp.sum(full * full, axis=1, keepdims=True)
    frob_norm = jnp.sqrt(jnp.sum(squares, axis=0, keepdims=True) + EPSILON)
    first = full * (1.0 / frob_norm)
    second = product(first, first)
    inner = second - 4.5 * first
    z_rest = (6.75 * second - 39.0 * first + product(inner, inner)) * (1.0 / 16.0)
    y_two = 2.25 * first + product(first, z_rest)
    q_rest = 4.5 * z_rest + product(z_rest, z_rest)
    z_three = (
        3.375 * identity + 1.5 * z_rest - 2.53125 * y_two - 0.5 * product(y_two, q_rest)
    )
    whitener = (z_three * (1.0 / jnp.sqrt(frob_norm))).astype(BF16)

    white_slab = dot(comp[...], whitener).astype(BF16)
    query_forward.wait_recv()
    for k in range(n_entity):
        query_f32[k * count : (k + 1) * count, :] = query_all[k].astype(F32)
    white_query = dot(query_f32[...].astype(BF16), whitener).astype(BF16)
    scores = lax.dot_general(
        white_query, white_slab, (((1,), (1,)), ((), ())), preferred_element_type=F32
    ) * width ** (-0.5)
    top = jnp.max(scores, axis=1, keepdims=True)
    weights = jnp.exp(scores - top)
    denom = jnp.sum(weights, axis=1, keepdims=True)
    lane = lax.broadcasted_iota(jnp.int32, (n_entity * count, LANES), 1)
    tail = jnp.zeros(lane.shape, F32)
    for number, part in enumerate(three_parts(top) + three_parts(denom)):
        tail = jnp.where(lane == number, part, tail)
    summed = dot(weights.astype(BF16), white_slab)
    for k in range(n_entity):
        part_send[k, :, :width] = summed[k * count : (k + 1) * count, :].astype(BF16)
        part_send[k, :, width:] = tail[k * count : (k + 1) * count, :].astype(BF16)
    for hop, peer in others:
        there = lax.rem(peer, 2) * half + peer // 2
        remote(part_send.at[there], part_recv.at[hop - 1], sems, 6, peer).start()
    wait_bytes(part_recv, recv_sem.at[6])
    parts = [part_send[my_slot]] + [part_recv[k] for k in range(n_entity - 1)]
    tails = [part[:, width:].astype(F32) for part in parts]
    tops = [t[:, 0:1] + t[:, 1:2] + t[:, 2:3] for t in tails]
    denoms = [t[:, 3:4] + t[:, 4:5] + t[:, 5:6] for t in tails]
    row_top = functools.reduce(jnp.maximum, tops)
    factors = [jnp.exp(t - row_top) for t in tops]
    denom_all = functools.reduce(jnp.add, [f * d for f, d in zip(factors, denoms)])
    result = functools.reduce(
        jnp.add, [f * part[:, :width].astype(F32) for f, part in zip(factors, parts)]
    )
    out_ref[...] = result / denom_all

    to_pair.wait_send()
    wait_bytes(gram_recv, send_sem.at[1])
    wait_bytes(query_all.at[pl.ds(0, half - 1)], send_sem.at[2])
    wait_bytes(gram_all.at[pl.ds(0, half - 1)], send_sem.at[3])
    gram_forward.wait_send()
    query_forward.wait_send()
    wait_bytes(part_recv, send_sem.at[6])


def solution(mesh):
    n_entity = mesh.shape["entity"]

    def per_device(companies, queries):
        rows, width = companies.shape
        count = queries.shape[0]
        n_blocks = width // LANES
        tiles = n_blocks * (n_blocks + 1) // 2 * (LANES // TILE)
        per_piece = -(-tiles // n_entity)
        return pl.pallas_call(
            functools.partial(kernel, n_entity),
            out_shape=jax.ShapeDtypeStruct((count, width), F32),
            in_specs=[
                pl.BlockSpec(memory_space=pltpu.HBM),
                pl.BlockSpec(memory_space=pltpu.HBM),
            ],
            out_specs=pl.BlockSpec(memory_space=pltpu.VMEM),
            scratch_shapes=[
                pltpu.VMEM((rows, width), BF16),
                pltpu.VMEM((n_entity, count, width), BF16),
                pltpu.VMEM((n_entity * count, width), F32),
                pltpu.VMEM((n_entity, per_piece, TILE, LANES), BF16),
                pltpu.VMEM((n_entity // 2, per_piece, TILE, LANES), BF16),
                pltpu.VMEM((n_entity // 2 - 1, per_piece, TILE, LANES), BF16),
                pltpu.VMEM((n_entity, per_piece, TILE, LANES), BF16),
                pltpu.VMEM((width, width), F32),
                pltpu.VMEM((n_entity, count, width + LANES), BF16),
                pltpu.VMEM((n_entity - 1, count, width + LANES), BF16),
                pltpu.SemaphoreType.DMA((2,)),
                pltpu.SemaphoreType.DMA((7,)),
                pltpu.SemaphoreType.DMA((7,)),
            ],
            compiler_params=pltpu.CompilerParams(
                collective_id=0, has_side_effects=True, vmem_limit_bytes=48 << 20
            ),
            name="whiten_pool",
        )(pltpu.with_memory_space_constraint(companies, pltpu.HBM), pltpu.with_memory_space_constraint(queries, pltpu.HBM))

    return jax.shard_map(
        per_device,
        mesh=mesh,
        in_specs=(P("entity", None), P(("news", "entity"), None)),
        out_specs=P(("news", "entity"), None),
        check_vma=False,
    )
```

```python
import functools

import jax
import jax.numpy as jnp
from jax import lax
from jax.experimental import pallas as pl
from jax.experimental.pallas import tpu as pltpu
from jax.sharding import PartitionSpec as P

RIDGE = 0.05
EPSILON = 1e-06
MESH = pl.DeviceIdType.MESH
LANES = 128
LOADS = 2
F32 = jnp.float32
BF16 = jnp.bfloat16


def dot(first_mat, second_mat):
    return jnp.dot(first_mat, second_mat, preferred_element_type=F32)


def product(first_mat, second_mat):
    return dot(first_mat.astype(BF16), second_mat.astype(BF16))


def remote(src_ref, dst_ref, sems, number, peer):
    send_sem, recv_sem = sems
    return pltpu.make_async_remote_copy(
        src_ref=src_ref,
        dst_ref=dst_ref,
        send_sem=send_sem.at[number],
        recv_sem=recv_sem.at[number],
        device_id={"entity": peer},
        device_id_type=MESH,
    )


def wait_bytes(ref, sem):
    pltpu.make_async_copy(ref, ref, sem).wait()


def flipped(chip, flip):
    bit, result = 1, chip
    while bit <= flip:
        if flip & bit:
            result = result + bit - 2 * bit * lax.rem(chip // bit, 2)
        bit *= 2
    return result


def packing(n_blocks):
    merged = [(i, i) for i in range(0, n_blocks, 2)]
    return merged, [(i, j) for i in range(n_blocks) for j in range(i + 1, n_blocks)]


def kernel(
    n_entity,
    comp_hbm,
    query_hbm,
    out_ref,
    comp,
    query_all,
    query_f32,
    gram_send,
    gram_pair,
    gram_recv,
    gram_all,
    diag_send,
    diag_recv,
    diag_sum,
    gram,
    part_send,
    part_recv,
    tail_send,
    tail_recv,
    tail_cols,
    load_sem,
    send_sem,
    recv_sem,
    ring_send,
    ring_recv,
    pass_send,
    pass_recv,
    hello,
):
    rows, width = comp.shape
    count = query_hbm.shape[0]
    total_rows = rows * n_entity
    n_blocks = width // LANES
    piece_rows = gram_send.shape[1]
    per_block = LANES // piece_rows
    me = lax.axis_index("entity")
    half = n_entity // 2
    chip, core = me // 2, lax.rem(me, 2)
    sibling = me + 1 - 2 * core
    my_slot = core * half + chip
    sems = (send_sem, recv_sem)
    flips = list(range(half - 1, 0, -1))

    barrier = pltpu.get_barrier_semaphore()

    @pl.when(core == 0)
    def _():
        pl.semaphore_signal(
            barrier, inc=1, device_id={"entity": sibling}, device_id_type=MESH
        )

    load_chunks = LOADS
    chunk = rows // load_chunks
    loads = [
        pltpu.make_async_copy(
            comp_hbm.at[pl.ds(c * chunk, chunk)],
            comp.at[pl.ds(c * chunk, chunk)],
            load_sem.at[c],
        )
        for c in range(load_chunks)
    ]
    for load in loads:
        load.start()
    load_query = pltpu.make_async_copy(
        query_hbm, query_all.at[my_slot], load_sem.at[load_chunks]
    )
    load_query.start()

    @pl.when(core == 1)
    def _():
        pl.semaphore_wait(barrier, 1)
        pl.semaphore_signal(
            hello, inc=1, device_id={"entity": sibling}, device_id_type=MESH
        )

    @pl.when(core == 0)
    def _():
        pl.semaphore_wait(hello, 1)
        for flip in flips:
            pl.semaphore_signal(
                barrier,
                inc=1,
                device_id={"entity": 2 * flipped(chip, flip)},
                device_id_type=MESH,
            )

    for load in loads:
        load.wait()
    merged, plain = packing(n_blocks)
    row_ids = lax.broadcasted_iota(jnp.int32, (LANES, LANES), 0)
    col_ids = lax.broadcasted_iota(jnp.int32, (LANES, LANES), 1)
    diagonals = {}
    items = merged + plain

    def pack(item, block):
        for t in range(per_block):
            gram_send[items.index(item) * per_block + t] = block[
                t * piece_rows : (t + 1) * piece_rows, :
            ].astype(BF16)

    for i in range(n_blocks):
        row_part = lax.dot_general(
            comp[:, i * LANES : (i + 1) * LANES],
            comp[:, i * LANES :],
            (((0,), (0,)), ((), ())),
            preferred_element_type=F32,
        )
        row_part = row_part * (1.0 / total_rows)
        diagonals[i] = row_part[:, :LANES]
        for j in range(i + 1, n_blocks):
            pack((i, j), row_part[:, (j - i) * LANES : (j - i + 1) * LANES])
        if i % 2:
            pack((i - 1, i - 1), jnp.where(row_ids <= col_ids, diagonals[i - 1], diagonals[i]))
            diag_send[i // 2 : i // 2 + 1, :] = jnp.sum(
                jnp.where(row_ids == col_ids, diagonals[i], 0.0), axis=0, keepdims=True
            )

    own_half = pl.ds(core * half, half)
    other_half = pl.ds((1 - core) * half, half)
    to_pair = remote(gram_send.at[other_half], gram_pair, sems, 0, sibling)
    to_pair.start()

    @pl.when(core == 0)
    def _():
        pl.semaphore_wait(barrier, half - 1)
        pl.semaphore_signal(
            hello, inc=1, device_id={"entity": sibling}, device_id_type=MESH
        )

    @pl.when(core == 1)
    def _():
        pl.semaphore_wait(hello, 1)

    load_query.wait()
    to_pair.wait_recv()
    for k in range(half):
        gram_pair[k] = (gram_pair[k].astype(F32) + gram_send[core * half + k].astype(F32)).astype(
            gram_pair.dtype
        )
    there = {flip: flipped(chip, flip) for flip in flips}
    for flip in flips:
        remote(
            gram_pair.at[there[flip]], gram_recv.at[flip - 1], sems, 1, 2 * there[flip] + core
        ).start()
    for flip in flips:
        remote(
            query_all.at[my_slot], query_all.at[my_slot], sems, 2, 2 * there[flip] + core
        ).start()
    for flip in flips:
        remote(diag_send, diag_recv.at[flip - 1], sems, 3, 2 * there[flip] + core).start()
    total = gram_pair[chip].astype(F32)
    wait_bytes(gram_recv, recv_sem.at[1])
    for k in range(half - 1):
        total = total + gram_recv[k].astype(F32)
    gram_all[my_slot] = total.astype(gram_all.dtype)

    def spread(number, peer, slot):
        return pltpu.make_async_remote_copy(
            src_ref=gram_all.at[slot],
            dst_ref=gram_all.at[slot],
            send_sem=ring_send.at[number],
            recv_sem=ring_recv.at[number],
            device_id={"entity": peer},
            device_id_type=MESH,
        )

    def forward(number, slot):
        return pltpu.make_async_remote_copy(
            src_ref=gram_all.at[slot],
            dst_ref=gram_all.at[slot],
            send_sem=pass_send.at[number],
            recv_sem=pass_recv.at[number],
            device_id={"entity": sibling},
            device_id_type=MESH,
        )

    for flip in flips:
        spread(flip, 2 * there[flip] + core, my_slot).start()
    forwards = [forward(0, my_slot)]
    forwards[0].start()
    wait_bytes(query_all.at[pl.ds(0, half - 1)], recv_sem.at[2])
    query_forward = remote(query_all.at[own_half], query_all.at[own_half], sems, 5, sibling)
    query_forward.start()
    wait_bytes(diag_recv, recv_sem.at[3])
    diag_total = diag_send[...]
    for k in range(half - 1):
        diag_total = diag_total + diag_recv[k]
    diag_sum[0] = diag_total
    diag_forward = remote(diag_sum.at[0], diag_sum.at[1], sems, 4, sibling)
    diag_forward.start()
    arrivals = sorted(flips, key=lambda flip: (bin(flip).count("1") + flip // 4, flip))
    for flip in arrivals:
        slot = core * half + there[flip]
        spread(flip, 2 * there[flip] + core, slot).wait_recv()
        forwards.append(forward(flip, slot))
        forwards[-1].start()
    diag_forward.wait_recv()
    for step in forwards:
        step.wait_recv()
    diag_rows = diag_sum[0] + diag_sum[1]

    for number, (i, j) in enumerate(items):
        block = (
            gram_all[number * per_block : (number + 1) * per_block]
            .astype(F32)
            .reshape(LANES, LANES)
        )
        turned = block.T
        at_i, at_j = slice(i * LANES, (i + 1) * LANES), slice(j * LANES, (j + 1) * LANES)
        if i != j:
            gram[at_i, at_j] = block
            gram[at_j, at_i] = turned
        else:
            at_j = slice((i + 1) * LANES, (i + 2) * LANES)
            gram[at_i, at_i] = jnp.where(row_ids <= col_ids, block, turned)
            second_block = jnp.where(row_ids > col_ids, block, turned)
            gram[at_j, at_j] = jnp.where(
                row_ids == col_ids, diag_rows[i // 2 : i // 2 + 1, :], second_block
            )

    row_ids = lax.broadcasted_iota(jnp.int32, (width, width), 0)
    col_ids = lax.broadcasted_iota(jnp.int32, (width, width), 1)
    identity = (row_ids == col_ids).astype(F32)
    full = gram[...] + RIDGE * identity
    squares = jnp.sum(full * full, axis=1, keepdims=True)
    frob_norm = jnp.sqrt(jnp.sum(squares, axis=0, keepdims=True) + EPSILON)
    first = full * (1.0 / frob_norm)
    second = product(first, first)
    inner = second - 4.5 * first
    z_rest = (6.75 * second - 39.0 * first + product(inner, inner)) * (1.0 / 16.0)
    y_two = 2.25 * first + product(first, z_rest)
    q_rest = 4.5 * z_rest + product(z_rest, z_rest)
    z_three = (
        3.375 * identity + 1.5 * z_rest - 2.53125 * y_two - 0.5 * product(y_two, q_rest)
    )
    whitener = (z_three * (1.0 / jnp.sqrt(frob_norm))).astype(BF16)

    white_slab = dot(comp[...], whitener).astype(BF16)
    query_forward.wait_recv()
    for k in range(n_entity):
        query_f32[k * count : (k + 1) * count, :] = query_all[k].astype(F32)
    white_query = dot(query_f32[...].astype(BF16), whitener).astype(BF16)
    scores = lax.dot_general(
        white_query, white_slab, (((1,), (1,)), ((), ())), preferred_element_type=F32
    ) * width ** (-0.5)
    top = jnp.max(scores, axis=1, keepdims=True)
    weights = jnp.exp(scores - top)
    denom = jnp.sum(weights, axis=1, keepdims=True)
    level = top + jnp.log(denom)
    level_row = jnp.broadcast_to(level, (n_entity * count, LANES)).T[0:1, :]
    tail_send[...] = level_row
    tail_recv[0] = level_row
    summed = dot(weights.astype(BF16), white_slab) * (1.0 / denom)
    for k in range(n_entity):
        part_send[k] = summed[k * count : (k + 1) * count, :].astype(BF16)
    others = [(flip, turn) for flip in flips + [0] for turn in (0, 1) if flip or turn]
    far_core = 1 - core
    for flip, turn in others:
        peer_chip = there[flip] if flip else chip
        peer_core = far_core if turn else core
        number = 2 * flip + turn
        peer = 2 * peer_chip + peer_core
        remote(tail_send, tail_recv.at[number], sems, 7, peer).start()
        remote(
            part_send.at[peer_core * half + peer_chip], part_recv.at[number - 1], sems, 6, peer
        ).start()
    wait_bytes(tail_recv.at[pl.ds(0, n_entity - 1)], recv_sem.at[7])
    levels = tail_recv[...].reshape(n_entity, n_entity * count)
    tail_cols[...] = levels.T
    mine = tail_cols[pl.ds(pl.multiple_of(my_slot * count, count), count), :]
    factors = jnp.exp(mine - jnp.max(mine, axis=1, keepdims=True))
    factors = factors * (1.0 / jnp.sum(factors, axis=1, keepdims=True))
    wait_bytes(part_recv, recv_sem.at[6])
    parts = [part_send[my_slot]] + [part_recv[k] for k in range(n_entity - 1)]
    out_ref[...] = functools.reduce(
        jnp.add, [factors[:, k : k + 1] * part.astype(F32) for k, part in enumerate(parts)]
    )

    to_pair.wait_send()
    wait_bytes(gram_recv, send_sem.at[1])
    wait_bytes(query_all.at[pl.ds(0, half - 1)], send_sem.at[2])
    wait_bytes(diag_recv, send_sem.at[3])
    for flip in flips:
        spread(flip, 2 * there[flip] + core, my_slot).wait_send()
    for step in forwards:
        step.wait_send()
    diag_forward.wait_send()
    query_forward.wait_send()
    wait_bytes(part_recv, send_sem.at[6])
    wait_bytes(tail_recv.at[pl.ds(0, n_entity - 1)], send_sem.at[7])


def solution(mesh):
    n_entity = mesh.shape["entity"]

    def per_device(companies, queries):
        rows, width = companies.shape
        count = queries.shape[0]
        half = n_entity // 2
        merged, plain = packing(width // LANES)
        piece_rows = (len(merged) + len(plain)) * LANES // n_entity
        return pl.pallas_call(
            functools.partial(kernel, n_entity),
            out_shape=jax.ShapeDtypeStruct((count, width), F32),
            in_specs=[
                pl.BlockSpec(memory_space=pltpu.HBM),
                pl.BlockSpec(memory_space=pltpu.HBM),
            ],
            out_specs=pl.BlockSpec(memory_space=pltpu.VMEM),
            scratch_shapes=[
                pltpu.VMEM((rows, width), BF16),
                pltpu.VMEM((n_entity, count, width), BF16),
                pltpu.VMEM((n_entity * count, width), F32),
                pltpu.VMEM((n_entity, piece_rows, LANES), BF16),
                pltpu.VMEM((half, piece_rows, LANES), BF16),
                pltpu.VMEM((half - 1, piece_rows, LANES), BF16),
                pltpu.VMEM((n_entity, piece_rows, LANES), BF16),
                pltpu.VMEM((len(merged), LANES), F32),
                pltpu.VMEM((half - 1, len(merged), LANES), F32),
                pltpu.VMEM((2, len(merged), LANES), F32),
                pltpu.VMEM((width, width), F32),
                pltpu.VMEM((n_entity, count, width), BF16),
                pltpu.VMEM((n_entity - 1, count, width), BF16),
                pltpu.VMEM((1, n_entity * count), F32),
                pltpu.VMEM((n_entity, 1, n_entity * count), F32),
                pltpu.VMEM((n_entity * count, n_entity), F32),
                pltpu.SemaphoreType.DMA((LOADS + 1,)),
                pltpu.SemaphoreType.DMA((8,)),
                pltpu.SemaphoreType.DMA((8,)),
                pltpu.SemaphoreType.DMA((half,)),
                pltpu.SemaphoreType.DMA((half,)),
                pltpu.SemaphoreType.DMA((half,)),
                pltpu.SemaphoreType.DMA((half,)),
                pltpu.SemaphoreType.REGULAR,
            ],
            compiler_params=pltpu.CompilerParams(
                collective_id=0, has_side_effects=True, vmem_limit_bytes=48 << 20
            ),
            name="whiten_pool",
        )(*[pltpu.with_memory_space_constraint(a, pltpu.HBM) for a in (companies, queries)])

    return jax.shard_map(
        per_device,
        mesh=mesh,
        in_specs=(P("entity", None), P(("news", "entity"), None)),
        out_specs=P(("news", "entity"), None),
        check_vma=False,
    )
```

```python
import functools

import jax
import jax.numpy as jnp
from jax import lax
from jax.experimental import pallas as pl
from jax.experimental.pallas import tpu as pltpu
from jax.sharding import PartitionSpec as P

RIDGE = 0.05
EPSILON = 1e-06
MESH = pl.DeviceIdType.MESH
LANES = 128
LOADS = 2
F32 = jnp.float32
BF16 = jnp.bfloat16


def dot(first_mat, second_mat):
    return jnp.dot(first_mat, second_mat, preferred_element_type=F32)


def product(first_mat, second_mat):
    return dot(first_mat.astype(BF16), second_mat.astype(BF16))


def remote(src_ref, dst_ref, sems, number, peer):
    send_sem, recv_sem = sems
    return pltpu.make_async_remote_copy(
        src_ref=src_ref,
        dst_ref=dst_ref,
        send_sem=send_sem.at[number],
        recv_sem=recv_sem.at[number],
        device_id={"entity": peer},
        device_id_type=MESH,
    )


def wait_bytes(ref, sem):
    pltpu.make_async_copy(ref, ref, sem).wait()


def flipped(chip, flip):
    bit, result = 1, chip
    while bit <= flip:
        if flip & bit:
            result = result + bit - 2 * bit * lax.rem(chip // bit, 2)
        bit *= 2
    return result


def packing(n_blocks):
    merged = [(i, i) for i in range(0, n_blocks, 2)]
    return merged, [(i, j) for i in range(n_blocks) for j in range(i + 1, n_blocks)]


def kernel(
    n_entity,
    comp_hbm,
    query_hbm,
    out_ref,
    comp,
    query_all,
    query_f32,
    gram_send,
    gram_pair,
    gram_recv,
    gram_all,
    diag_send,
    diag_recv,
    diag_sum,
    gram,
    part_send,
    part_recv,
    tail_send,
    tail_recv,
    tail_cols,
    load_sem,
    send_sem,
    recv_sem,
    ring_send,
    ring_recv,
    pass_send,
    pass_recv,
    hello,
):
    rows, width = comp.shape
    count = query_hbm.shape[0]
    total_rows = rows * n_entity
    n_blocks = width // LANES
    piece_rows = gram_send.shape[1]
    per_block = LANES // piece_rows
    me = lax.axis_index("entity")
    half = n_entity // 2
    chip, core = me // 2, lax.rem(me, 2)
    sibling = me + 1 - 2 * core
    my_slot = core * half + chip
    sems = (send_sem, recv_sem)
    flips = list(range(half - 1, 0, -1))

    barrier = pltpu.get_barrier_semaphore()

    @pl.when(core == 0)
    def _():
        pl.semaphore_signal(
            barrier, inc=1, device_id={"entity": sibling}, device_id_type=MESH
        )

    load_chunks = LOADS
    chunk = rows // load_chunks
    loads = [
        pltpu.make_async_copy(
            comp_hbm.at[pl.ds(c * chunk, chunk)],
            comp.at[pl.ds(c * chunk, chunk)],
            load_sem.at[c],
        )
        for c in range(load_chunks)
    ]
    for load in loads:
        load.start()
    load_query = pltpu.make_async_copy(
        query_hbm, query_all.at[my_slot], load_sem.at[load_chunks]
    )
    load_query.start()

    @pl.when(core == 1)
    def _():
        pl.semaphore_wait(barrier, 1)
        pl.semaphore_signal(
            hello, inc=1, device_id={"entity": sibling}, device_id_type=MESH
        )

    @pl.when(core == 0)
    def _():
        pl.semaphore_wait(hello, 1)
        for flip in flips:
            pl.semaphore_signal(
                barrier,
                inc=1,
                device_id={"entity": 2 * flipped(chip, flip)},
                device_id_type=MESH,
            )

    for load in loads:
        load.wait()
    merged, plain = packing(n_blocks)
    row_ids = lax.broadcasted_iota(jnp.int32, (LANES, LANES), 0)
    col_ids = lax.broadcasted_iota(jnp.int32, (LANES, LANES), 1)
    diagonals = {}
    items = merged + plain

    def pack(item, block):
        for t in range(per_block):
            gram_send[items.index(item) * per_block + t] = block[
                t * piece_rows : (t + 1) * piece_rows, :
            ].astype(BF16)

    for i in range(n_blocks):
        row_part = lax.dot_general(
            comp[:, i * LANES : (i + 1) * LANES],
            comp[:, i * LANES :],
            (((0,), (0,)), ((), ())),
            preferred_element_type=F32,
        )
        row_part = row_part * (1.0 / total_rows)
        diagonals[i] = row_part[:, :LANES]
        for j in range(i + 1, n_blocks):
            pack((i, j), row_part[:, (j - i) * LANES : (j - i + 1) * LANES])
        if i % 2:
            pack((i - 1, i - 1), jnp.where(row_ids <= col_ids, diagonals[i - 1], diagonals[i]))
            diag_send[i // 2 : i // 2 + 1, :] = jnp.sum(
                jnp.where(row_ids == col_ids, diagonals[i], 0.0), axis=0, keepdims=True
            )

    own_half = pl.ds(core * half, half)
    other_half = pl.ds((1 - core) * half, half)
    to_pair = remote(gram_send.at[other_half], gram_pair, sems, 0, sibling)
    to_pair.start()

    @pl.when(core == 0)
    def _():
        pl.semaphore_wait(barrier, half - 1)
        pl.semaphore_signal(
            hello, inc=1, device_id={"entity": sibling}, device_id_type=MESH
        )

    @pl.when(core == 1)
    def _():
        pl.semaphore_wait(hello, 1)

    load_query.wait()
    to_pair.wait_recv()
    for k in range(half):
        gram_pair[k] = (gram_pair[k].astype(F32) + gram_send[core * half + k].astype(F32)).astype(
            gram_pair.dtype
        )
    there = {flip: flipped(chip, flip) for flip in flips}
    for flip in flips:
        remote(
            gram_pair.at[there[flip]], gram_recv.at[flip - 1], sems, 1, 2 * there[flip] + core
        ).start()
    for flip in flips:
        remote(
            query_all.at[my_slot], query_all.at[my_slot], sems, 2, 2 * there[flip] + core
        ).start()
    for flip in flips:
        remote(diag_send, diag_recv.at[flip - 1], sems, 3, 2 * there[flip] + core).start()
    total = gram_pair[chip].astype(F32)
    wait_bytes(gram_recv, recv_sem.at[1])
    for k in range(half - 1):
        total = total + gram_recv[k].astype(F32)
    gram_all[my_slot] = total.astype(gram_all.dtype)

    def spread(number, peer, slot):
        return pltpu.make_async_remote_copy(
            src_ref=gram_all.at[slot],
            dst_ref=gram_all.at[slot],
            send_sem=ring_send.at[number],
            recv_sem=ring_recv.at[number],
            device_id={"entity": peer},
            device_id_type=MESH,
        )

    def forward(number, slot):
        return pltpu.make_async_remote_copy(
            src_ref=gram_all.at[slot],
            dst_ref=gram_all.at[slot],
            send_sem=pass_send.at[number],
            recv_sem=pass_recv.at[number],
            device_id={"entity": sibling},
            device_id_type=MESH,
        )

    for flip in flips:
        spread(flip, 2 * there[flip] + core, my_slot).start()
    forwards = [forward(0, my_slot)]
    forwards[0].start()
    wait_bytes(query_all.at[pl.ds(0, half - 1)], recv_sem.at[2])
    query_forward = remote(query_all.at[own_half], query_all.at[own_half], sems, 5, sibling)
    query_forward.start()
    wait_bytes(diag_recv, recv_sem.at[3])
    diag_total = diag_send[...]
    for k in range(half - 1):
        diag_total = diag_total + diag_recv[k]
    diag_sum[0] = diag_total
    diag_forward = remote(diag_sum.at[0], diag_sum.at[1], sems, 4, sibling)
    diag_forward.start()
    arrivals = sorted(flips, key=lambda flip: (bin(flip).count("1") + flip // 4, flip))
    for flip in arrivals:
        slot = core * half + there[flip]
        spread(flip, 2 * there[flip] + core, slot).wait_recv()
        forwards.append(forward(flip, slot))
        forwards[-1].start()
    diag_forward.wait_recv()
    for step in forwards:
        step.wait_recv()
    diag_rows = diag_sum[0] + diag_sum[1]

    for number, (i, j) in enumerate(items):
        block = (
            gram_all[number * per_block : (number + 1) * per_block]
            .astype(F32)
            .reshape(LANES, LANES)
        )
        turned = block.T
        at_i, at_j = slice(i * LANES, (i + 1) * LANES), slice(j * LANES, (j + 1) * LANES)
        if i != j:
            gram[at_i, at_j] = block
            gram[at_j, at_i] = turned
        else:
            at_j = slice((i + 1) * LANES, (i + 2) * LANES)
            gram[at_i, at_i] = jnp.where(row_ids <= col_ids, block, turned)
            second_block = jnp.where(row_ids > col_ids, block, turned)
            gram[at_j, at_j] = jnp.where(
                row_ids == col_ids, diag_rows[i // 2 : i // 2 + 1, :], second_block
            )

    row_ids = lax.broadcasted_iota(jnp.int32, (width, width), 0)
    col_ids = lax.broadcasted_iota(jnp.int32, (width, width), 1)
    identity = (row_ids == col_ids).astype(F32)
    full = gram[...] + RIDGE * identity
    squares = jnp.sum(full * full, axis=1, keepdims=True)
    frob_norm = jnp.sqrt(jnp.sum(squares, axis=0, keepdims=True) + EPSILON)
    first = full * (1.0 / frob_norm)
    second = product(first, first)
    inner = second - 4.5 * first
    z_rest = (6.75 * second - 39.0 * first + product(inner, inner)) * (1.0 / 16.0)
    y_two = 2.25 * first + product(first, z_rest)
    q_rest = 4.5 * z_rest + product(z_rest, z_rest)
    z_three = (
        3.375 * identity + 1.5 * z_rest - 2.53125 * y_two - 0.5 * product(y_two, q_rest)
    )
    whitener = (z_three * (1.0 / jnp.sqrt(frob_norm))).astype(BF16)

    white_slab = dot(comp[...], whitener).astype(BF16)
    query_forward.wait_recv()
    for k in range(n_entity):
        query_f32[k * count : (k + 1) * count, :] = query_all[k].astype(F32)
    white_query = dot(query_f32[...].astype(BF16), whitener).astype(BF16)
    scores = lax.dot_general(
        white_query, white_slab, (((1,), (1,)), ((), ())), preferred_element_type=F32
    ) * width ** (-0.5)
    top = jnp.max(scores, axis=1, keepdims=True)
    weights = jnp.exp(scores - top)
    denom = jnp.sum(weights, axis=1, keepdims=True)
    level = top + jnp.log(denom)
    level_row = jnp.broadcast_to(level, (n_entity * count, LANES)).T[0:1, :]
    tail_send[...] = level_row
    tail_recv[my_slot] = level_row
    summed = dot(weights.astype(BF16), white_slab) * (1.0 / denom)
    for k in range(n_entity):
        part_send[k] = summed[k * count : (k + 1) * count, :].astype(BF16)
    for k in range(n_entity - 1):
        peer = k + (k >= me).astype(jnp.int32)
        remote(tail_send, tail_recv.at[my_slot], sems, 7, peer).start()
        peer_slot = lax.rem(peer, 2) * half + peer // 2
        remote(part_send.at[peer_slot], part_recv.at[my_slot], sems, 6, peer).start()
    wait_bytes(tail_recv.at[pl.ds(0, n_entity - 1)], recv_sem.at[7])
    levels = tail_recv[...].reshape(n_entity, n_entity * count)
    tail_cols[...] = levels.T
    mine = tail_cols[pl.ds(pl.multiple_of(my_slot * count, count), count), :]
    factors = jnp.exp(mine - jnp.max(mine, axis=1, keepdims=True))
    factors = factors * (1.0 / jnp.sum(factors, axis=1, keepdims=True))
    wait_bytes(part_recv.at[pl.ds(0, n_entity - 1)], recv_sem.at[6])
    part_recv[my_slot] = part_send[my_slot]
    parts = [part_recv[k] for k in range(n_entity)]
    out_ref[...] = functools.reduce(
        jnp.add, [factors[:, k : k + 1] * part.astype(F32) for k, part in enumerate(parts)]
    )

    to_pair.wait_send()
    wait_bytes(gram_recv, send_sem.at[1])
    wait_bytes(query_all.at[pl.ds(0, half - 1)], send_sem.at[2])
    wait_bytes(diag_recv, send_sem.at[3])
    for flip in flips:
        spread(flip, 2 * there[flip] + core, my_slot).wait_send()
    for step in forwards:
        step.wait_send()
    diag_forward.wait_send()
    query_forward.wait_send()
    wait_bytes(part_recv.at[pl.ds(0, n_entity - 1)], send_sem.at[6])
    wait_bytes(tail_recv.at[pl.ds(0, n_entity - 1)], send_sem.at[7])


def solution(mesh):
    n_entity = mesh.shape["entity"]

    def per_device(companies, queries):
        rows, width = companies.shape
        count = queries.shape[0]
        half = n_entity // 2
        merged, plain = packing(width // LANES)
        piece_rows = (len(merged) + len(plain)) * LANES // n_entity
        return pl.pallas_call(
            functools.partial(kernel, n_entity),
            out_shape=jax.ShapeDtypeStruct((count, width), F32),
            in_specs=[
                pl.BlockSpec(memory_space=pltpu.HBM),
                pl.BlockSpec(memory_space=pltpu.HBM),
            ],
            out_specs=pl.BlockSpec(memory_space=pltpu.VMEM),
            scratch_shapes=[
                pltpu.VMEM((rows, width), BF16),
                pltpu.VMEM((n_entity, count, width), BF16),
                pltpu.VMEM((n_entity * count, width), F32),
                pltpu.VMEM((n_entity, piece_rows, LANES), BF16),
                pltpu.VMEM((half, piece_rows, LANES), BF16),
                pltpu.VMEM((half - 1, piece_rows, LANES), BF16),
                pltpu.VMEM((n_entity, piece_rows, LANES), BF16),
                pltpu.VMEM((len(merged), LANES), F32),
                pltpu.VMEM((half - 1, len(merged), LANES), F32),
                pltpu.VMEM((2, len(merged), LANES), F32),
                pltpu.VMEM((width, width), F32),
                pltpu.VMEM((n_entity, count, width), BF16),
                pltpu.VMEM((n_entity, count, width), BF16),
                pltpu.VMEM((1, n_entity * count), F32),
                pltpu.VMEM((n_entity, 1, n_entity * count), F32),
                pltpu.VMEM((n_entity * count, n_entity), F32),
                pltpu.SemaphoreType.DMA((LOADS + 1,)),
                pltpu.SemaphoreType.DMA((8,)),
                pltpu.SemaphoreType.DMA((8,)),
                pltpu.SemaphoreType.DMA((half,)),
                pltpu.SemaphoreType.DMA((half,)),
                pltpu.SemaphoreType.DMA((half,)),
                pltpu.SemaphoreType.DMA((half,)),
                pltpu.SemaphoreType.REGULAR,
            ],
            compiler_params=pltpu.CompilerParams(
                collective_id=0, has_side_effects=True, vmem_limit_bytes=48 << 20
            ),
            name="whiten_pool",
        )(*[pltpu.with_memory_space_constraint(a, pltpu.HBM) for a in (companies, queries)])

    return jax.shard_map(
        per_device,
        mesh=mesh,
        in_specs=(P("entity", None), P(("news", "entity"), None)),
        out_specs=P(("news", "entity"), None),
        check_vma=False,
    )
```

```python
import functools

import jax
import jax.numpy as jnp
from jax import lax
from jax.experimental import pallas as pl
from jax.experimental.pallas import tpu as pltpu
from jax.sharding import PartitionSpec as P

RIDGE = 0.05
EPSILON = 1e-06
MESH = pl.DeviceIdType.MESH
LANES = 128
LOADS = 2
SLABS = 4
F32 = jnp.float32
BF16 = jnp.bfloat16


def dot(first_mat, second_mat):
    return jnp.dot(first_mat, second_mat, preferred_element_type=F32)


def upper_product(first_mat, second_mat):
    middle = first_mat.shape[0] // 2
    return (
        dot(first_mat[:middle, :], second_mat),
        dot(first_mat[middle:, :], second_mat[:, middle:]),
    )


def mirrored(parts):
    top, corner = (part.astype(BF16) for part in parts)
    middle = top.shape[0]
    bottom = jnp.concatenate([top[:, middle:].T, corner], axis=1)
    return jnp.concatenate([top, bottom], axis=0)


def add_unit(part, unit):
    rows = []
    for i in range(part.shape[0] // LANES):
        at = slice(i * LANES, (i + 1) * LANES)
        pieces = [part[at, : i * LANES], part[at, at] + unit, part[at, (i + 1) * LANES :]]
        rows.append(jnp.concatenate([piece for piece in pieces if piece.shape[1]], axis=1))
    return jnp.concatenate(rows, axis=0)


def remote(src_ref, dst_ref, sems, number, peer):
    send_sem, recv_sem = sems
    return pltpu.make_async_remote_copy(
        src_ref=src_ref,
        dst_ref=dst_ref,
        send_sem=send_sem.at[number],
        recv_sem=recv_sem.at[number],
        device_id={"entity": peer},
        device_id_type=MESH,
    )


def wait_bytes(ref, sem):
    pltpu.make_async_copy(ref, ref, sem).wait()


def flipped(chip, flip):
    bit, result = 1, chip
    while bit <= flip:
        if flip & bit:
            result = result + bit - 2 * bit * lax.rem(chip // bit, 2)
        bit *= 2
    return result


def packing(n_blocks):
    merged = [(i, i) for i in range(0, n_blocks, 2)]
    return merged, [(i, j) for i in range(n_blocks) for j in range(i + 1, n_blocks)]


def kernel(
    n_entity,
    comp_hbm,
    query_hbm,
    out_ref,
    comp,
    query_all,
    gram_send,
    gram_pair,
    gram_recv,
    gram_all,
    diag_send,
    diag_recv,
    diag_sum,
    gram,
    gram_low,
    part_send,
    part_recv,
    tail_send,
    tail_recv,
    tail_cols,
    load_sem,
    send_sem,
    recv_sem,
    ring_send,
    ring_recv,
    pass_send,
    pass_recv,
    hello,
):
    rows, width = comp.shape
    count = query_hbm.shape[0]
    total_rows = rows * n_entity
    n_blocks = width // LANES
    piece_rows = gram_send.shape[1]
    per_block = LANES // piece_rows
    me = lax.axis_index("entity")
    half = n_entity // 2
    chip, core = me // 2, lax.rem(me, 2)
    sibling = me + 1 - 2 * core
    my_slot = core * half + chip
    sems = (send_sem, recv_sem)
    flips = list(range(half - 1, 0, -1))

    barrier = pltpu.get_barrier_semaphore()

    @pl.when(core == 0)
    def _():
        pl.semaphore_signal(
            barrier, inc=1, device_id={"entity": sibling}, device_id_type=MESH
        )

    load_chunks = LOADS
    chunk = rows // load_chunks
    loads = [
        pltpu.make_async_copy(
            comp_hbm.at[pl.ds(c * chunk, chunk)],
            comp.at[pl.ds(c * chunk, chunk)],
            load_sem.at[c],
        )
        for c in range(load_chunks)
    ]
    for load in loads:
        load.start()
    load_query = pltpu.make_async_copy(
        query_hbm, query_all.at[my_slot], load_sem.at[load_chunks]
    )
    load_query.start()

    @pl.when(core == 1)
    def _():
        pl.semaphore_wait(barrier, 1)
        pl.semaphore_signal(
            hello, inc=1, device_id={"entity": sibling}, device_id_type=MESH
        )

    @pl.when(core == 0)
    def _():
        pl.semaphore_wait(hello, 1)
        for flip in flips:
            pl.semaphore_signal(
                barrier,
                inc=1,
                device_id={"entity": 2 * flipped(chip, flip)},
                device_id_type=MESH,
            )

    for load in loads:
        load.wait()
    merged, plain = packing(n_blocks)
    row_ids = lax.broadcasted_iota(jnp.int32, (LANES, LANES), 0)
    col_ids = lax.broadcasted_iota(jnp.int32, (LANES, LANES), 1)
    diagonals = {}
    items = merged + plain

    def pack(item, block):
        for t in range(per_block):
            gram_send[items.index(item) * per_block + t] = block[
                t * piece_rows : (t + 1) * piece_rows, :
            ].astype(BF16)

    for i in range(n_blocks):
        row_part = lax.dot_general(
            comp[:, i * LANES : (i + 1) * LANES],
            comp[:, i * LANES :],
            (((0,), (0,)), ((), ())),
            preferred_element_type=F32,
        )
        row_part = row_part * (1.0 / total_rows)
        diagonals[i] = row_part[:, :LANES]
        for j in range(i + 1, n_blocks):
            pack((i, j), row_part[:, (j - i) * LANES : (j - i + 1) * LANES])
        if i % 2:
            pack((i - 1, i - 1), jnp.where(row_ids <= col_ids, diagonals[i - 1], diagonals[i]))
            diag_send[i // 2 : i // 2 + 1, :] = jnp.sum(
                jnp.where(row_ids == col_ids, diagonals[i], 0.0), axis=0, keepdims=True
            )

    own_half = pl.ds(core * half, half)
    other_half = pl.ds((1 - core) * half, half)
    to_pair = remote(gram_send.at[other_half], gram_pair, sems, 0, sibling)
    to_pair.start()

    @pl.when(core == 0)
    def _():
        pl.semaphore_wait(barrier, half - 1)
        pl.semaphore_signal(
            hello, inc=1, device_id={"entity": sibling}, device_id_type=MESH
        )

    @pl.when(core == 1)
    def _():
        pl.semaphore_wait(hello, 1)

    load_query.wait()
    to_pair.wait_recv()
    for k in range(half):
        gram_pair[k] = (gram_pair[k].astype(F32) + gram_send[core * half + k].astype(F32)).astype(
            gram_pair.dtype
        )
    there = {flip: flipped(chip, flip) for flip in flips}
    for flip in flips:
        remote(
            gram_pair.at[there[flip]], gram_recv.at[flip - 1], sems, 1, 2 * there[flip] + core
        ).start()
    for flip in flips:
        remote(
            query_all.at[my_slot], query_all.at[my_slot], sems, 2, 2 * there[flip] + core
        ).start()
    for flip in flips:
        remote(diag_send, diag_recv.at[flip - 1], sems, 3, 2 * there[flip] + core).start()
    total = gram_pair[chip].astype(F32)
    wait_bytes(gram_recv, recv_sem.at[1])
    for k in range(half - 1):
        total = total + gram_recv[k].astype(F32)
    gram_all[my_slot] = total.astype(gram_all.dtype)

    def spread(number, peer, slot):
        return pltpu.make_async_remote_copy(
            src_ref=gram_all.at[slot],
            dst_ref=gram_all.at[slot],
            send_sem=ring_send,
            recv_sem=ring_recv.at[number],
            device_id={"entity": peer},
            device_id_type=MESH,
        )

    def forward(number, slot):
        return pltpu.make_async_remote_copy(
            src_ref=gram_all.at[slot],
            dst_ref=gram_all.at[slot],
            send_sem=pass_send.at[number],
            recv_sem=pass_recv.at[number],
            device_id={"entity": sibling},
            device_id_type=MESH,
        )

    for q in range(half - 1, 0, -1):
        peer = q - (q <= chip).astype(jnp.int32)
        spread(chip, 2 * peer + core, my_slot).start()
    forwards = [forward(0, my_slot)]
    forwards[0].start()
    wait_bytes(query_all.at[pl.ds(0, half - 1)], recv_sem.at[2])
    query_forward = remote(query_all.at[own_half], query_all.at[own_half], sems, 5, sibling)
    query_forward.start()
    wait_bytes(diag_recv, recv_sem.at[3])
    diag_total = diag_send[...]
    for k in range(half - 1):
        diag_total = diag_total + diag_recv[k]
    diag_sum[0] = diag_total
    diag_forward = remote(diag_sum.at[0], diag_sum.at[1], sems, 4, sibling)
    diag_forward.start()
    arrivals = sorted(flips, key=lambda flip: (bin(flip).count("1") + flip // 4, flip))
    for flip in arrivals:
        slot = core * half + there[flip]
        spread(there[flip], 2 * there[flip] + core, slot).wait_recv()
        forwards.append(forward(flip, slot))
        forwards[-1].start()
    diag_forward.wait_recv()
    for step in forwards:
        step.wait_recv()
    diag_rows = diag_sum[0] + diag_sum[1]

    ridge = jnp.where(row_ids == col_ids, RIDGE, 0.0)
    squares = jnp.zeros((LANES, LANES), F32)

    def place(i, j, value):
        at = (slice(i * LANES, (i + 1) * LANES), slice(j * LANES, (j + 1) * LANES))
        if i < n_blocks // 2 or j >= n_blocks // 2:
            gram[at] = value
        gram_low[at] = value.astype(BF16)

    for number, (i, j) in enumerate(items):
        block = (
            gram_all[number * per_block : (number + 1) * per_block]
            .astype(F32)
            .reshape(LANES, LANES)
        )
        turned = block.T
        if i != j:
            place(i, j, block)
            place(j, i, turned)
            squares = squares + 2.0 * (block * block)
        else:
            even = jnp.where(row_ids <= col_ids, block, turned) + ridge
            odd = jnp.where(row_ids > col_ids, block, turned)
            odd = jnp.where(row_ids == col_ids, diag_rows[i // 2 : i // 2 + 1, :], odd) + ridge
            place(i, i, even)
            place(i + 1, i + 1, odd)
            squares = squares + even * even + odd * odd

    squares = jnp.sum(squares, axis=0, keepdims=True)
    frob_square = jnp.sum(squares, axis=1, keepdims=True) + EPSILON
    frob_norm = jnp.sqrt(frob_square)
    inverse = 1.0 / frob_norm
    inverse_square = inverse * inverse
    root = 1.0 / jnp.sqrt(frob_norm)
    middle = width // 2
    low = gram_low[...]
    full = (gram[:middle, :], gram[middle:, middle:])
    second = upper_product(low, low)
    inner = mirrored([a - (4.5 * frob_norm) * b for a, b in zip(second, full)])
    fourth = upper_product(inner, inner)
    z_rest = [
        (0.421875 * inverse_square) * a
        - (2.4375 * inverse) * b
        + (0.0625 * inverse_square * inverse_square) * c
        for a, b, c in zip(second, full, fourth)
    ]
    z_low = mirrored(z_rest)
    y_two = [2.25 * a + b for a, b in zip(full, upper_product(low, z_low))]
    y_low = mirrored(y_two)
    q_low = mirrored([4.5 * a + b for a, b in zip(z_rest, upper_product(z_low, z_low))])
    last = upper_product(y_low, q_low)
    z_three = [
        (1.5 * root) * a - (inverse * root) * (2.53125 * b + 0.5 * c)
        for a, b, c in zip(z_rest, y_two, last)
    ]
    unit = jnp.where(row_ids == col_ids, 3.375 * root, 0.0)
    whitener = mirrored([add_unit(part, unit) for part in z_three])

    query_forward.wait_recv()
    query_block = query_all[...].astype(F32).reshape(n_entity * count, width).astype(BF16)
    white_query = dot(query_block, whitener).astype(BF16)
    score_scale = width ** (-0.5)
    slab_chunk = rows // SLABS
    slabs = [
        dot(comp[c * slab_chunk : (c + 1) * slab_chunk, :], whitener).astype(BF16)
        for c in range(SLABS)
    ]
    scores = [
        lax.dot_general(
            white_query, slab, (((1,), (1,)), ((), ())), preferred_element_type=F32
        )
        for slab in slabs
    ]
    tops = [jnp.max(part, axis=1, keepdims=True) for part in scores]
    weights = [jnp.exp((part - top) * score_scale) for part, top in zip(scores, tops)]
    denoms = [jnp.sum(part, axis=1, keepdims=True) for part in weights]
    sums = [dot(part.astype(BF16), slab) for part, slab in zip(weights, slabs)]
    top = functools.reduce(jnp.maximum, tops)
    scales = [jnp.exp((part - top) * score_scale) for part in tops]
    denom = functools.reduce(jnp.add, [a * b for a, b in zip(scales, denoms)])
    level = top * score_scale + jnp.log(denom)
    level_row = jnp.broadcast_to(level, (n_entity * count, LANES)).T[0:1, :]
    tail_send[...] = level_row
    tail_recv[my_slot] = level_row
    share = 1.0 / denom
    summed = functools.reduce(jnp.add, [(a * share) * b for a, b in zip(scales, sums)])
    for k in range(n_entity):
        part_send[k] = summed[k * count : (k + 1) * count, :].astype(BF16)
    for k in range(n_entity - 1):
        peer = k + (k >= me).astype(jnp.int32)
        remote(tail_send, tail_recv.at[my_slot], sems, 7, peer).start()
        peer_slot = lax.rem(peer, 2) * half + peer // 2
        remote(part_send.at[peer_slot], part_recv.at[my_slot], sems, 6, peer).start()
    wait_bytes(tail_recv.at[pl.ds(0, n_entity - 1)], recv_sem.at[7])
    levels = tail_recv[...].reshape(n_entity, n_entity * count)
    tail_cols[...] = levels.T
    mine = tail_cols[pl.ds(pl.multiple_of(my_slot * count, count), count), :]
    factors = jnp.exp(mine - jnp.max(mine, axis=1, keepdims=True))
    factors = factors * (1.0 / jnp.sum(factors, axis=1, keepdims=True))
    wait_bytes(part_recv.at[pl.ds(0, n_entity - 1)], recv_sem.at[6])
    part_recv[my_slot] = part_send[my_slot]
    parts = [part_recv[k] for k in range(n_entity)]
    out_ref[...] = functools.reduce(
        jnp.add, [factors[:, k : k + 1] * part.astype(F32) for k, part in enumerate(parts)]
    )

    to_pair.wait_send()
    wait_bytes(gram_recv, send_sem.at[1])
    wait_bytes(query_all.at[pl.ds(0, half - 1)], send_sem.at[2])
    wait_bytes(diag_recv, send_sem.at[3])
    for _ in range(half - 1):
        spread(chip, 2 * there[1] + core, my_slot).wait_send()
    for step in forwards:
        step.wait_send()
    diag_forward.wait_send()
    query_forward.wait_send()
    wait_bytes(part_recv.at[pl.ds(0, n_entity - 1)], send_sem.at[6])
    wait_bytes(tail_recv.at[pl.ds(0, n_entity - 1)], send_sem.at[7])


def solution(mesh):
    n_entity = mesh.shape["entity"]

    def per_device(companies, queries):
        rows, width = companies.shape
        count = queries.shape[0]
        half = n_entity // 2
        merged, plain = packing(width // LANES)
        piece_rows = (len(merged) + len(plain)) * LANES // n_entity
        return pl.pallas_call(
            functools.partial(kernel, n_entity),
            out_shape=jax.ShapeDtypeStruct((count, width), F32),
            in_specs=[
                pl.BlockSpec(memory_space=pltpu.HBM),
                pl.BlockSpec(memory_space=pltpu.HBM),
            ],
            out_specs=pl.BlockSpec(memory_space=pltpu.VMEM),
            scratch_shapes=[
                pltpu.VMEM((rows, width), BF16),
                pltpu.VMEM((n_entity, count, width), BF16),
                pltpu.VMEM((n_entity, piece_rows, LANES), BF16),
                pltpu.VMEM((half, piece_rows, LANES), BF16),
                pltpu.VMEM((half - 1, piece_rows, LANES), BF16),
                pltpu.VMEM((n_entity, piece_rows, LANES), BF16),
                pltpu.VMEM((len(merged), LANES), F32),
                pltpu.VMEM((half - 1, len(merged), LANES), F32),
                pltpu.VMEM((2, len(merged), LANES), F32),
                pltpu.VMEM((width, width), F32),
                pltpu.VMEM((width, width), BF16),
                pltpu.VMEM((n_entity, count, width), BF16),
                pltpu.VMEM((n_entity, count, width), BF16),
                pltpu.VMEM((1, n_entity * count), F32),
                pltpu.VMEM((n_entity, 1, n_entity * count), F32),
                pltpu.VMEM((n_entity * count, n_entity), F32),
                pltpu.SemaphoreType.DMA((LOADS + 1,)),
                pltpu.SemaphoreType.DMA((8,)),
                pltpu.SemaphoreType.DMA((8,)),
                pltpu.SemaphoreType.DMA,
                pltpu.SemaphoreType.DMA((half,)),
                pltpu.SemaphoreType.DMA((half,)),
                pltpu.SemaphoreType.DMA((half,)),
                pltpu.SemaphoreType.REGULAR,
            ],
            compiler_params=pltpu.CompilerParams(
                collective_id=0, has_side_effects=True, vmem_limit_bytes=48 << 20
            ),
            name="whiten_pool",
        )(*[pltpu.with_memory_space_constraint(a, pltpu.HBM) for a in (companies, queries)])

    return jax.shard_map(
        per_device,
        mesh=mesh,
        in_specs=(P("entity", None), P(("news", "entity"), None)),
        out_specs=P(("news", "entity"), None),
        check_vma=False,
    )
```

```python
import functools

import jax
import jax.numpy as jnp
from jax import lax
from jax.experimental import pallas as pl
from jax.experimental.pallas import tpu as pltpu
from jax.sharding import PartitionSpec as P

RIDGE = 0.05
EPSILON = 1e-06
MESH = pl.DeviceIdType.MESH
LANES = 128
LOADS = 2
TILE = 16
EVEN = 2
SLABS = 4
F32 = jnp.float32
BF16 = jnp.bfloat16


def dot(first_mat, second_mat):
    return jnp.dot(first_mat, second_mat, preferred_element_type=F32)


def upper_product(first_mat, second_mat):
    middle = first_mat.shape[0] // 2
    return (
        dot(first_mat[:middle, :], second_mat),
        dot(first_mat[middle:, :], second_mat[:, middle:]),
    )


def mirrored(parts):
    top, corner = (part.astype(BF16) for part in parts)
    middle = top.shape[0]
    bottom = jnp.concatenate([top[:, middle:].T, corner], axis=1)
    return jnp.concatenate([top, bottom], axis=0)


def add_unit(part, unit):
    rows = []
    for i in range(part.shape[0] // LANES):
        at = slice(i * LANES, (i + 1) * LANES)
        pieces = [part[at, : i * LANES], part[at, at] + unit, part[at, (i + 1) * LANES :]]
        rows.append(jnp.concatenate([piece for piece in pieces if piece.shape[1]], axis=1))
    return jnp.concatenate(rows, axis=0)


def remote(src_ref, dst_ref, sems, number, peer):
    send_sem, recv_sem = sems
    return pltpu.make_async_remote_copy(
        src_ref=src_ref,
        dst_ref=dst_ref,
        send_sem=send_sem.at[number],
        recv_sem=recv_sem.at[number],
        device_id={"entity": peer},
        device_id_type=MESH,
    )


def wait_bytes(ref, sem):
    pltpu.make_async_copy(ref, ref, sem).wait()


def flipped(chip, flip):
    bit, result = 1, chip
    while bit <= flip:
        if flip & bit:
            result = result + bit - 2 * bit * lax.rem(chip // bit, 2)
        bit *= 2
    return result


def core_shares(tiles, half):
    both = tiles // half
    first = max(1, both * EVEN // 8)
    return (0, first), (half * first, both - first)


def packing(n_blocks):
    merged = [(i, i) for i in range(0, n_blocks, 2)]
    return merged, [(i, j) for i in range(n_blocks) for j in range(i + 1, n_blocks)]


def kernel(
    n_entity,
    comp_hbm,
    query_hbm,
    out_ref,
    comp,
    query_all,
    gram_send,
    gram_pair,
    gram_recv,
    gram_all,
    diag_send,
    diag_recv,
    diag_sum,
    gram,
    gram_low,
    part_send,
    part_recv,
    tail_send,
    tail_recv,
    tail_cols,
    load_sem,
    send_sem,
    recv_sem,
    ring_send,
    ring_recv,
    pass_send,
    pass_recv,
    hello,
):
    rows, width = comp.shape
    count = query_hbm.shape[0]
    total_rows = rows * n_entity
    n_blocks = width // LANES
    per_block = LANES // TILE
    me = lax.axis_index("entity")
    half = n_entity // 2
    chip, core = me // 2, lax.rem(me, 2)
    sibling = me + 1 - 2 * core
    my_slot = core * half + chip
    sems = (send_sem, recv_sem)
    flips = list(range(half - 1, 0, -1))
    shares = core_shares(gram_send.shape[0], half)

    barrier = pltpu.get_barrier_semaphore()

    @pl.when(core == 1)
    def _():
        pl.semaphore_signal(
            barrier, inc=1, device_id={"entity": sibling}, device_id_type=MESH
        )

    load_chunks = LOADS
    chunk = rows // load_chunks
    loads = [
        pltpu.make_async_copy(
            comp_hbm.at[pl.ds(c * chunk, chunk)],
            comp.at[pl.ds(c * chunk, chunk)],
            load_sem.at[c],
        )
        for c in range(load_chunks)
    ]
    for load in loads:
        load.start()
    load_query = pltpu.make_async_copy(
        query_hbm, query_all.at[my_slot], load_sem.at[load_chunks]
    )
    load_query.start()

    @pl.when(core == 0)
    def _():
        pl.semaphore_wait(barrier, 1)
        pl.semaphore_signal(
            hello, inc=1, device_id={"entity": sibling}, device_id_type=MESH
        )

    @pl.when(core == 1)
    def _():
        pl.semaphore_wait(hello, 1)
        for flip in flips:
            pl.semaphore_signal(
                barrier,
                inc=1,
                device_id={"entity": 2 * flipped(chip, flip) + 1},
                device_id_type=MESH,
            )

    for load in loads:
        load.wait()
    merged, plain = packing(n_blocks)
    row_ids = lax.broadcasted_iota(jnp.int32, (LANES, LANES), 0)
    col_ids = lax.broadcasted_iota(jnp.int32, (LANES, LANES), 1)
    diagonals = {}
    items = merged + plain

    def pack(item, block):
        for t in range(per_block):
            gram_send[items.index(item) * per_block + t] = block[
                t * TILE : (t + 1) * TILE, :
            ].astype(BF16)

    for i in range(n_blocks):
        row_part = lax.dot_general(
            comp[:, i * LANES : (i + 1) * LANES],
            comp[:, i * LANES :],
            (((0,), (0,)), ((), ())),
            preferred_element_type=F32,
        )
        row_part = row_part * (1.0 / total_rows)
        diagonals[i] = row_part[:, :LANES]
        for j in range(i + 1, n_blocks):
            pack((i, j), row_part[:, (j - i) * LANES : (j - i + 1) * LANES])
        if i % 2:
            pack((i - 1, i - 1), jnp.where(row_ids <= col_ids, diagonals[i - 1], diagonals[i]))
            diag_send[i // 2 : i // 2 + 1, :] = jnp.sum(
                jnp.where(row_ids == col_ids, diagonals[i], 0.0), axis=0, keepdims=True
            )

    own_half = pl.ds(core * half, half)
    def to_pair(side):
        base, share = shares[1 - side]
        return pltpu.make_async_remote_copy(
            src_ref=gram_send.at[pl.ds(base, half * share)],
            dst_ref=gram_pair.at[pl.ds(0, half * share)],
            send_sem=send_sem.at[0],
            recv_sem=recv_sem.at[0],
            device_id={"entity": sibling},
            device_id_type=MESH,
        )

    def by_core(step):
        pl.when(core == 0)(functools.partial(step, 0))
        pl.when(core == 1)(functools.partial(step, 1))

    by_core(lambda side: to_pair(side).start())

    @pl.when(core == 1)
    def _():
        pl.semaphore_wait(barrier, half - 1)
        pl.semaphore_signal(
            hello, inc=1, device_id={"entity": sibling}, device_id_type=MESH
        )

    @pl.when(core == 0)
    def _():
        pl.semaphore_wait(hello, 1)

    load_query.wait()
    there = {flip: flipped(chip, flip) for flip in flips}

    def scatter(side):
        base, share = shares[side]
        to_pair(1 - side).wait_recv()
        gram_pair[: half * share] = (
            gram_pair[: half * share].astype(F32)
            + gram_send[base : base + half * share].astype(F32)
        ).astype(gram_pair.dtype)
        for number, flip in enumerate(flips):
            remote(
                gram_pair.at[pl.ds(there[flip] * share, share)],
                gram_recv.at[pl.ds(number * share, share)],
                sems,
                1,
                2 * there[flip] + core,
            ).start()

    by_core(scatter)
    for flip in flips:
        remote(
            query_all.at[my_slot], query_all.at[my_slot], sems, 2, 2 * there[flip] + core
        ).start()
    for flip in flips:
        remote(diag_send, diag_recv.at[flip - 1], sems, 3, 2 * there[flip] + core).start()

    def piece(side, owner):
        base, share = shares[side]
        return gram_all.at[pl.ds(base + owner * share, share)]

    def spread(side, owner, peer):
        return pltpu.make_async_remote_copy(
            src_ref=piece(side, owner),
            dst_ref=piece(side, owner),
            send_sem=ring_send,
            recv_sem=ring_recv.at[owner],
            device_id={"entity": 2 * peer + side},
            device_id_type=MESH,
        )

    def forward(side, number, owner):
        return pltpu.make_async_remote_copy(
            src_ref=piece(side, owner),
            dst_ref=piece(side, owner),
            send_sem=pass_send.at[number],
            recv_sem=pass_recv.at[number],
            device_id={"entity": sibling},
            device_id_type=MESH,
        )

    def gather(side):
        base, share = shares[side]
        arrived = gram_recv.at[pl.ds(0, (half - 1) * share)]
        wait_bytes(arrived, recv_sem.at[1])
        total = gram_pair[pl.ds(chip * share, share)].astype(F32)
        for k in range(half - 1):
            total = total + gram_recv[k * share : (k + 1) * share].astype(F32)
        gram_all[pl.ds(base + chip * share, share)] = total.astype(gram_all.dtype)
        for q in range(half - 1, 0, -1):
            peer = q - (q <= chip).astype(jnp.int32)
            spread(side, chip, peer).start()
        forward(side, 0, chip).start()

    by_core(gather)
    wait_bytes(diag_recv, recv_sem.at[3])
    diag_total = diag_send[...]
    for k in range(half - 1):
        diag_total = diag_total + diag_recv[k]
    diag_sum[0] = diag_total
    diag_forward = remote(diag_sum.at[0], diag_sum.at[1], sems, 4, sibling)
    diag_forward.start()
    arrivals = sorted(flips, key=lambda flip: (bin(flip).count("1") + flip // 4, flip))

    def pass_on(side):
        for flip in arrivals:
            spread(side, there[flip], there[flip]).wait_recv()
            forward(side, flip, there[flip]).start()

    by_core(pass_on)
    wait_bytes(query_all.at[pl.ds(0, half - 1)], recv_sem.at[2])
    query_forward = remote(query_all.at[own_half], query_all.at[own_half], sems, 5, sibling)
    query_forward.start()
    diag_forward.wait_recv()

    def passed(side):
        for flip in [0] + arrivals:
            forward(1 - side, flip, chip).wait_recv()

    by_core(passed)
    diag_rows = diag_sum[0] + diag_sum[1]

    ridge = jnp.where(row_ids == col_ids, RIDGE, 0.0)
    squares = jnp.zeros((LANES, LANES), F32)

    def place(i, j, value):
        at = (slice(i * LANES, (i + 1) * LANES), slice(j * LANES, (j + 1) * LANES))
        if i < n_blocks // 2 or j >= n_blocks // 2:
            gram[at] = value
        gram_low[at] = value.astype(BF16)

    for number, (i, j) in enumerate(items):
        block = (
            gram_all[number * per_block : (number + 1) * per_block]
            .astype(F32)
            .reshape(LANES, LANES)
        )
        turned = block.T
        if i != j:
            place(i, j, block)
            place(j, i, turned)
            squares = squares + 2.0 * (block * block)
        else:
            even = jnp.where(row_ids <= col_ids, block, turned) + ridge
            odd = jnp.where(row_ids > col_ids, block, turned)
            odd = jnp.where(row_ids == col_ids, diag_rows[i // 2 : i // 2 + 1, :], odd) + ridge
            place(i, i, even)
            place(i + 1, i + 1, odd)
            squares = squares + even * even + odd * odd

    squares = jnp.sum(squares, axis=0, keepdims=True)
    frob_square = jnp.sum(squares, axis=1, keepdims=True) + EPSILON
    frob_norm = jnp.sqrt(frob_square)
    inverse = 1.0 / frob_norm
    inverse_square = inverse * inverse
    root = 1.0 / jnp.sqrt(frob_norm)
    middle = width // 2
    low = gram_low[...]
    full = (gram[:middle, :], gram[middle:, middle:])
    second = upper_product(low, low)
    inner = mirrored([a - (4.5 * frob_norm) * b for a, b in zip(second, full)])
    fourth = upper_product(inner, inner)
    z_rest = [
        (0.421875 * inverse_square) * a
        - (2.4375 * inverse) * b
        + (0.0625 * inverse_square * inverse_square) * c
        for a, b, c in zip(second, full, fourth)
    ]
    z_low = mirrored(z_rest)
    y_two = [2.25 * a + b for a, b in zip(full, upper_product(low, z_low))]
    y_low = mirrored(y_two)
    q_low = mirrored([4.5 * a + b for a, b in zip(z_rest, upper_product(z_low, z_low))])
    last = upper_product(y_low, q_low)
    z_three = [
        (1.5 * root) * a - (inverse * root) * (2.53125 * b + 0.5 * c)
        for a, b, c in zip(z_rest, y_two, last)
    ]
    unit = jnp.where(row_ids == col_ids, 3.375 * root, 0.0)
    whitener = mirrored([add_unit(part, unit) for part in z_three])

    query_forward.wait_recv()
    query_block = query_all[...].astype(F32).reshape(n_entity * count, width).astype(BF16)
    white_query = dot(query_block, whitener).astype(BF16)
    score_scale = width ** (-0.5)
    slab_chunk = rows // SLABS
    slabs = [
        dot(comp[c * slab_chunk : (c + 1) * slab_chunk, :], whitener).astype(BF16)
        for c in range(SLABS)
    ]
    scores = [
        lax.dot_general(
            white_query, slab, (((1,), (1,)), ((), ())), preferred_element_type=F32
        )
        for slab in slabs
    ]
    tops = [jnp.max(part, axis=1, keepdims=True) for part in scores]
    weights = [jnp.exp((part - top) * score_scale) for part, top in zip(scores, tops)]
    denoms = [jnp.sum(part, axis=1, keepdims=True) for part in weights]
    sums = [dot(part.astype(BF16), slab) for part, slab in zip(weights, slabs)]
    top = functools.reduce(jnp.maximum, tops)
    scales = [jnp.exp((part - top) * score_scale) for part in tops]
    denom = functools.reduce(jnp.add, [a * b for a, b in zip(scales, denoms)])
    level = top * score_scale + jnp.log(denom)
    level_row = jnp.broadcast_to(level, (n_entity * count, LANES)).T[0:1, :]
    tail_send[...] = level_row
    tail_recv[my_slot] = level_row
    share = 1.0 / denom
    summed = functools.reduce(jnp.add, [(a * share) * b for a, b in zip(scales, sums)])
    for k in range(n_entity):
        part_send[k] = summed[k * count : (k + 1) * count, :].astype(BF16)
    for k in range(n_entity - 1):
        peer = k + (k >= me).astype(jnp.int32)
        remote(tail_send, tail_recv.at[my_slot], sems, 7, peer).start()
        peer_slot = lax.rem(peer, 2) * half + peer // 2
        remote(part_send.at[peer_slot], part_recv.at[my_slot], sems, 6, peer).start()
    wait_bytes(tail_recv.at[pl.ds(0, n_entity - 1)], recv_sem.at[7])
    levels = tail_recv[...].reshape(n_entity, n_entity * count)
    tail_cols[...] = levels.T
    mine = tail_cols[pl.ds(pl.multiple_of(my_slot * count, count), count), :]
    factors = jnp.exp(mine - jnp.max(mine, axis=1, keepdims=True))
    factors = factors * (1.0 / jnp.sum(factors, axis=1, keepdims=True))
    wait_bytes(part_recv.at[pl.ds(0, n_entity - 1)], recv_sem.at[6])
    part_recv[my_slot] = part_send[my_slot]
    parts = [part_recv[k] for k in range(n_entity)]
    out_ref[...] = functools.reduce(
        jnp.add, [factors[:, k : k + 1] * part.astype(F32) for k, part in enumerate(parts)]
    )

    def sent(side):
        share = shares[side][1]
        to_pair(side).wait_send()
        wait_bytes(gram_recv.at[pl.ds(0, (half - 1) * share)], send_sem.at[1])
        for _ in range(half - 1):
            spread(side, chip, chip).wait_send()
        for flip in [0] + arrivals:
            forward(side, flip, chip).wait_send()

    by_core(sent)
    wait_bytes(query_all.at[pl.ds(0, half - 1)], send_sem.at[2])
    wait_bytes(diag_recv, send_sem.at[3])
    diag_forward.wait_send()
    query_forward.wait_send()
    wait_bytes(part_recv.at[pl.ds(0, n_entity - 1)], send_sem.at[6])
    wait_bytes(tail_recv.at[pl.ds(0, n_entity - 1)], send_sem.at[7])


def solution(mesh):
    n_entity = mesh.shape["entity"]

    def per_device(companies, queries):
        rows, width = companies.shape
        count = queries.shape[0]
        half = n_entity // 2
        merged, plain = packing(width // LANES)
        tiles = (len(merged) + len(plain)) * LANES // TILE
        largest = max(share for _, share in core_shares(tiles, half))
        return pl.pallas_call(
            functools.partial(kernel, n_entity),
            out_shape=jax.ShapeDtypeStruct((count, width), F32),
            in_specs=[
                pl.BlockSpec(memory_space=pltpu.HBM),
                pl.BlockSpec(memory_space=pltpu.HBM),
            ],
            out_specs=pl.BlockSpec(memory_space=pltpu.VMEM),
            scratch_shapes=[
                pltpu.VMEM((rows, width), BF16),
                pltpu.VMEM((n_entity, count, width), BF16),
                pltpu.VMEM((tiles, TILE, LANES), BF16),
                pltpu.VMEM((half * largest, TILE, LANES), BF16),
                pltpu.VMEM(((half - 1) * largest, TILE, LANES), BF16),
                pltpu.VMEM((tiles, TILE, LANES), BF16),
                pltpu.VMEM((len(merged), LANES), F32),
                pltpu.VMEM((half - 1, len(merged), LANES), F32),
                pltpu.VMEM((2, len(merged), LANES), F32),
                pltpu.VMEM((width, width), F32),
                pltpu.VMEM((width, width), BF16),
                pltpu.VMEM((n_entity, count, width), BF16),
                pltpu.VMEM((n_entity, count, width), BF16),
                pltpu.VMEM((1, n_entity * count), F32),
                pltpu.VMEM((n_entity, 1, n_entity * count), F32),
                pltpu.VMEM((n_entity * count, n_entity), F32),
                pltpu.SemaphoreType.DMA((LOADS + 1,)),
                pltpu.SemaphoreType.DMA((8,)),
                pltpu.SemaphoreType.DMA((8,)),
                pltpu.SemaphoreType.DMA,
                pltpu.SemaphoreType.DMA((half,)),
                pltpu.SemaphoreType.DMA((half,)),
                pltpu.SemaphoreType.DMA((half,)),
                pltpu.SemaphoreType.REGULAR,
            ],
            compiler_params=pltpu.CompilerParams(
                collective_id=0, has_side_effects=True, vmem_limit_bytes=48 << 20
            ),
            name="whiten_pool",
        )(*[pltpu.with_memory_space_constraint(a, pltpu.HBM) for a in (companies, queries)])

    return jax.shard_map(
        per_device,
        mesh=mesh,
        in_specs=(P("entity", None), P(("news", "entity"), None)),
        out_specs=P(("news", "entity"), None),
        check_vma=False,
    )
```

```python
import functools

import jax
import jax.numpy as jnp
from jax import lax
from jax.experimental import pallas as pl
from jax.experimental.pallas import tpu as pltpu
from jax.sharding import PartitionSpec as P

RIDGE = 0.05
EPSILON = 1e-06
MESH = pl.DeviceIdType.MESH
LANES = 128
LOADS = 2
TILE = 16
EVEN = 2
SLABS = 4
F32 = jnp.float32
BF16 = jnp.bfloat16


def dot(first_mat, second_mat):
    return jnp.dot(first_mat, second_mat, preferred_element_type=F32)


def upper_product(first_mat, second_mat):
    middle = first_mat.shape[0] // 2
    return (
        dot(first_mat[:middle, :], second_mat),
        dot(first_mat[middle:, :], second_mat[:, middle:]),
    )


def mirrored(parts):
    top, corner = (part.astype(BF16) for part in parts)
    middle = top.shape[0]
    bottom = jnp.concatenate([top[:, middle:].T, corner], axis=1)
    return jnp.concatenate([top, bottom], axis=0)


def add_unit(part, unit):
    rows = []
    for i in range(part.shape[0] // LANES):
        at = slice(i * LANES, (i + 1) * LANES)
        pieces = [part[at, : i * LANES], part[at, at] + unit, part[at, (i + 1) * LANES :]]
        rows.append(jnp.concatenate([piece for piece in pieces if piece.shape[1]], axis=1))
    return jnp.concatenate(rows, axis=0)


def remote(src_ref, dst_ref, sems, number, peer):
    send_sem, recv_sem = sems
    return pltpu.make_async_remote_copy(
        src_ref=src_ref,
        dst_ref=dst_ref,
        send_sem=send_sem.at[number],
        recv_sem=recv_sem.at[number],
        device_id={"entity": peer},
        device_id_type=MESH,
    )


def wait_bytes(ref, sem):
    pltpu.make_async_copy(ref, ref, sem).wait()


def flipped(chip, flip):
    bit, result = 1, chip
    while bit <= flip:
        if flip & bit:
            result = result + bit - 2 * bit * lax.rem(chip // bit, 2)
        bit *= 2
    return result


def core_shares(tiles, half):
    both = tiles // half
    first = max(1, both * EVEN // 8)
    return (0, first), (half * first, both - first)


def packing(n_blocks):
    merged = [(i, i) for i in range(0, n_blocks, 2)]
    return merged, [(i, j) for i in range(n_blocks) for j in range(i + 1, n_blocks)]


def kernel(
    n_entity,
    comp_hbm,
    query_hbm,
    out_ref,
    comp,
    query_all,
    gram_send,
    gram_pair,
    gram_recv,
    gram_all,
    diag_send,
    diag_recv,
    diag_sum,
    gram,
    gram_low,
    part_send,
    part_recv,
    tail_send,
    tail_recv,
    tail_cols,
    load_sem,
    send_sem,
    recv_sem,
    ring_send,
    ring_recv,
    pass_send,
    pass_recv,
    hello,
):
    rows, width = comp.shape
    count = query_hbm.shape[0]
    total_rows = rows * n_entity
    n_blocks = width // LANES
    per_block = LANES // TILE
    me = lax.axis_index("entity")
    half = n_entity // 2
    chip, core = me // 2, lax.rem(me, 2)
    sibling = me + 1 - 2 * core
    my_slot = core * half + chip
    sems = (send_sem, recv_sem)
    flips = list(range(half - 1, 0, -1))
    shares = core_shares(gram_send.shape[0], half)

    barrier = pltpu.get_barrier_semaphore()

    @pl.when(core == 1)
    def _():
        pl.semaphore_signal(
            barrier, inc=1, device_id={"entity": sibling}, device_id_type=MESH
        )

    load_chunks = LOADS
    chunk = rows // load_chunks
    loads = [
        pltpu.make_async_copy(
            comp_hbm.at[pl.ds(c * chunk, chunk)],
            comp.at[pl.ds(c * chunk, chunk)],
            load_sem.at[c],
        )
        for c in range(load_chunks)
    ]
    for load in loads:
        load.start()
    load_query = pltpu.make_async_copy(
        query_hbm, query_all.at[my_slot], load_sem.at[load_chunks]
    )
    load_query.start()

    @pl.when(core == 0)
    def _():
        pl.semaphore_wait(barrier, 1)
        pl.semaphore_signal(
            hello, inc=1, device_id={"entity": sibling}, device_id_type=MESH
        )

    @pl.when(core == 1)
    def _():
        pl.semaphore_wait(hello, 1)
        for flip in flips:
            pl.semaphore_signal(
                barrier,
                inc=1,
                device_id={"entity": 2 * flipped(chip, flip) + 1},
                device_id_type=MESH,
            )

    for load in loads:
        load.wait()
    merged, plain = packing(n_blocks)
    row_ids = lax.broadcasted_iota(jnp.int32, (LANES, LANES), 0)
    col_ids = lax.broadcasted_iota(jnp.int32, (LANES, LANES), 1)
    diagonals = {}
    items = merged + plain

    def pack(item, block):
        for t in range(per_block):
            gram_send[items.index(item) * per_block + t] = block[
                t * TILE : (t + 1) * TILE, :
            ].astype(BF16)

    for i in range(n_blocks):
        row_part = lax.dot_general(
            comp[:, i * LANES : (i + 1) * LANES],
            comp[:, i * LANES :],
            (((0,), (0,)), ((), ())),
            preferred_element_type=F32,
        )
        row_part = row_part * (1.0 / total_rows)
        diagonals[i] = row_part[:, :LANES]
        for j in range(i + 1, n_blocks):
            pack((i, j), row_part[:, (j - i) * LANES : (j - i + 1) * LANES])
        if i % 2:
            pack((i - 1, i - 1), jnp.where(row_ids <= col_ids, diagonals[i - 1], diagonals[i]))
            diag_send[i // 2 : i // 2 + 1, :] = jnp.sum(
                jnp.where(row_ids == col_ids, diagonals[i], 0.0), axis=0, keepdims=True
            )

    own_half = pl.ds(core * half, half)
    def to_pair(side):
        base, share = shares[1 - side]
        return pltpu.make_async_remote_copy(
            src_ref=gram_send.at[pl.ds(base, half * share)],
            dst_ref=gram_pair.at[pl.ds(0, half * share)],
            send_sem=send_sem.at[0],
            recv_sem=recv_sem.at[0],
            device_id={"entity": sibling},
            device_id_type=MESH,
        )

    def by_core(step):
        pl.when(core == 0)(functools.partial(step, 0))
        pl.when(core == 1)(functools.partial(step, 1))

    by_core(lambda side: to_pair(side).start())

    @pl.when(core == 1)
    def _():
        pl.semaphore_wait(barrier, half - 1)
        pl.semaphore_signal(
            hello, inc=1, device_id={"entity": sibling}, device_id_type=MESH
        )

    @pl.when(core == 0)
    def _():
        pl.semaphore_wait(hello, 1)

    load_query.wait()
    there = {flip: flipped(chip, flip) for flip in flips}

    def scatter(side):
        base, share = shares[side]
        to_pair(1 - side).wait_recv()
        gram_pair[: half * share] = (
            gram_pair[: half * share].astype(F32)
            + gram_send[base : base + half * share].astype(F32)
        ).astype(gram_pair.dtype)
        for q in range(half - 1):
            peer = q + (q >= chip).astype(jnp.int32)
            number = chip - (chip > peer).astype(jnp.int32)
            remote(
                gram_pair.at[pl.ds(peer * share, share)],
                gram_recv.at[pl.ds(number * share, share)],
                sems,
                1,
                2 * peer + core,
            ).start()

    by_core(scatter)
    for flip in flips:
        remote(
            query_all.at[my_slot], query_all.at[my_slot], sems, 2, 2 * there[flip] + core
        ).start()
    for flip in flips:
        remote(diag_send, diag_recv.at[flip - 1], sems, 3, 2 * there[flip] + core).start()

    def piece(side, owner):
        base, share = shares[side]
        return gram_all.at[pl.ds(base + owner * share, share)]

    def spread(side, owner, peer):
        return pltpu.make_async_remote_copy(
            src_ref=piece(side, owner),
            dst_ref=piece(side, owner),
            send_sem=ring_send,
            recv_sem=ring_recv.at[owner],
            device_id={"entity": 2 * peer + side},
            device_id_type=MESH,
        )

    def forward(side, number, owner):
        return pltpu.make_async_remote_copy(
            src_ref=piece(side, owner),
            dst_ref=piece(side, owner),
            send_sem=pass_send.at[number],
            recv_sem=pass_recv.at[number],
            device_id={"entity": sibling},
            device_id_type=MESH,
        )

    def gather(side):
        base, share = shares[side]
        arrived = gram_recv.at[pl.ds(0, (half - 1) * share)]
        wait_bytes(arrived, recv_sem.at[1])
        total = gram_pair[pl.ds(chip * share, share)].astype(F32)
        for k in range(half - 1):
            total = total + gram_recv[k * share : (k + 1) * share].astype(F32)
        gram_all[pl.ds(base + chip * share, share)] = total.astype(gram_all.dtype)
        for q in range(half - 1, 0, -1):
            peer = q - (q <= chip).astype(jnp.int32)
            spread(side, chip, peer).start()
        forward(side, 0, chip).start()

    by_core(gather)
    wait_bytes(diag_recv, recv_sem.at[3])
    diag_total = diag_send[...]
    for k in range(half - 1):
        diag_total = diag_total + diag_recv[k]
    diag_sum[0] = diag_total
    diag_forward = remote(diag_sum.at[0], diag_sum.at[1], sems, 4, sibling)
    diag_forward.start()
    arrivals = sorted(flips, key=lambda flip: (bin(flip).count("1") + flip // 4, flip))

    def pass_on(side):
        for flip in arrivals:
            spread(side, there[flip], there[flip]).wait_recv()
            forward(side, flip, there[flip]).start()

    by_core(pass_on)
    wait_bytes(query_all.at[pl.ds(0, half - 1)], recv_sem.at[2])
    query_forward = remote(query_all.at[own_half], query_all.at[own_half], sems, 5, sibling)
    query_forward.start()
    diag_forward.wait_recv()

    def passed(side):
        for flip in [0] + arrivals:
            forward(1 - side, flip, chip).wait_recv()

    by_core(passed)
    diag_rows = diag_sum[0] + diag_sum[1]

    ridge = jnp.where(row_ids == col_ids, RIDGE, 0.0)
    squares = jnp.zeros((LANES, LANES), F32)

    def place(i, j, value):
        at = (slice(i * LANES, (i + 1) * LANES), slice(j * LANES, (j + 1) * LANES))
        if i < n_blocks // 2 or j >= n_blocks // 2:
            gram[at] = value
        gram_low[at] = value.astype(BF16)

    for number, (i, j) in enumerate(items):
        block = (
            gram_all[number * per_block : (number + 1) * per_block]
            .astype(F32)
            .reshape(LANES, LANES)
        )
        turned = block.T
        if i != j:
            place(i, j, block)
            place(j, i, turned)
            squares = squares + 2.0 * (block * block)
        else:
            even = jnp.where(row_ids <= col_ids, block, turned) + ridge
            odd = jnp.where(row_ids > col_ids, block, turned)
            odd = jnp.where(row_ids == col_ids, diag_rows[i // 2 : i // 2 + 1, :], odd) + ridge
            place(i, i, even)
            place(i + 1, i + 1, odd)
            squares = squares + even * even + odd * odd

    squares = jnp.sum(squares, axis=0, keepdims=True)
    frob_square = jnp.sum(squares, axis=1, keepdims=True) + EPSILON
    frob_norm = jnp.sqrt(frob_square)
    inverse = 1.0 / frob_norm
    inverse_square = inverse * inverse
    root = 1.0 / jnp.sqrt(frob_norm)
    middle = width // 2
    low = gram_low[...]
    full = (gram[:middle, :], gram[middle:, middle:])
    second = upper_product(low, low)
    inner = mirrored([a - (4.5 * frob_norm) * b for a, b in zip(second, full)])
    fourth = upper_product(inner, inner)
    z_rest = [
        (0.421875 * inverse_square) * a
        - (2.4375 * inverse) * b
        + (0.0625 * inverse_square * inverse_square) * c
        for a, b, c in zip(second, full, fourth)
    ]
    z_low = mirrored(z_rest)
    y_two = [2.25 * a + b for a, b in zip(full, upper_product(low, z_low))]
    y_low = mirrored(y_two)
    q_low = mirrored([4.5 * a + b for a, b in zip(z_rest, upper_product(z_low, z_low))])
    last = upper_product(y_low, q_low)
    z_three = [
        (1.5 * root) * a - (inverse * root) * (2.53125 * b + 0.5 * c)
        for a, b, c in zip(z_rest, y_two, last)
    ]
    unit = jnp.where(row_ids == col_ids, 3.375 * root, 0.0)
    whitener = mirrored([add_unit(part, unit) for part in z_three])

    query_forward.wait_recv()
    query_block = query_all[...].astype(F32).reshape(n_entity * count, width).astype(BF16)
    white_query = dot(query_block, whitener).astype(BF16)
    score_scale = width ** (-0.5)
    slab_chunk = rows // SLABS
    slabs = [
        dot(comp[c * slab_chunk : (c + 1) * slab_chunk, :], whitener).astype(BF16)
        for c in range(SLABS)
    ]
    scores = [
        lax.dot_general(
            white_query, slab, (((1,), (1,)), ((), ())), preferred_element_type=F32
        )
        for slab in slabs
    ]
    tops = [jnp.max(part, axis=1, keepdims=True) for part in scores]
    weights = [jnp.exp((part - top) * score_scale) for part, top in zip(scores, tops)]
    denoms = [jnp.sum(part, axis=1, keepdims=True) for part in weights]
    sums = [dot(part.astype(BF16), slab) for part, slab in zip(weights, slabs)]
    top = functools.reduce(jnp.maximum, tops)
    scales = [jnp.exp((part - top) * score_scale) for part in tops]
    denom = functools.reduce(jnp.add, [a * b for a, b in zip(scales, denoms)])
    level = top * score_scale + jnp.log(denom)
    level_row = jnp.broadcast_to(level, (n_entity * count, LANES)).T[0:1, :]
    tail_send[...] = level_row
    tail_recv[my_slot] = level_row
    for k in range(n_entity - 1):
        peer = k + (k >= me).astype(jnp.int32)
        remote(tail_send, tail_recv.at[my_slot], sems, 7, peer).start()
    share = 1.0 / denom
    summed = functools.reduce(jnp.add, [(a * share) * b for a, b in zip(scales, sums)])
    for k in range(n_entity):
        part_send[k] = summed[k * count : (k + 1) * count, :].astype(BF16)
    for k in range(n_entity - 1):
        peer = k + (k >= me).astype(jnp.int32)
        peer_slot = lax.rem(peer, 2) * half + peer // 2
        remote(part_send.at[peer_slot], part_recv.at[my_slot], sems, 6, peer).start()
    def sent(side):
        share = shares[side][1]
        to_pair(side).wait_send()
        wait_bytes(gram_recv.at[pl.ds(0, (half - 1) * share)], send_sem.at[1])
        for _ in range(half - 1):
            spread(side, chip, chip).wait_send()
        for flip in [0] + arrivals:
            forward(side, flip, chip).wait_send()

    by_core(sent)
    wait_bytes(query_all.at[pl.ds(0, half - 1)], send_sem.at[2])
    wait_bytes(diag_recv, send_sem.at[3])
    diag_forward.wait_send()
    query_forward.wait_send()
    wait_bytes(part_recv.at[pl.ds(0, n_entity - 1)], send_sem.at[6])
    wait_bytes(tail_recv.at[pl.ds(0, n_entity - 1)], send_sem.at[7])
    wait_bytes(tail_recv.at[pl.ds(0, n_entity - 1)], recv_sem.at[7])
    levels = tail_recv[...].reshape(n_entity, n_entity * count)
    tail_cols[...] = levels.T
    mine = tail_cols[pl.ds(pl.multiple_of(my_slot * count, count), count), :]
    factors = jnp.exp(mine - jnp.max(mine, axis=1, keepdims=True))
    factors = factors * (1.0 / jnp.sum(factors, axis=1, keepdims=True))
    wait_bytes(part_recv.at[pl.ds(0, n_entity - 1)], recv_sem.at[6])
    part_recv[my_slot] = part_send[my_slot]
    parts = [part_recv[k] for k in range(n_entity)]
    out_ref[...] = functools.reduce(
        jnp.add, [factors[:, k : k + 1] * part.astype(F32) for k, part in enumerate(parts)]
    )


def solution(mesh):
    n_entity = mesh.shape["entity"]

    def per_device(companies, queries):
        rows, width = companies.shape
        count = queries.shape[0]
        half = n_entity // 2
        merged, plain = packing(width // LANES)
        tiles = (len(merged) + len(plain)) * LANES // TILE
        largest = max(share for _, share in core_shares(tiles, half))
        return pl.pallas_call(
            functools.partial(kernel, n_entity),
            out_shape=jax.ShapeDtypeStruct((count, width), F32),
            in_specs=[
                pl.BlockSpec(memory_space=pltpu.HBM),
                pl.BlockSpec(memory_space=pltpu.HBM),
            ],
            out_specs=pl.BlockSpec(memory_space=pltpu.VMEM),
            scratch_shapes=[
                pltpu.VMEM((rows, width), BF16),
                pltpu.VMEM((n_entity, count, width), BF16),
                pltpu.VMEM((tiles, TILE, LANES), BF16),
                pltpu.VMEM((half * largest, TILE, LANES), BF16),
                pltpu.VMEM(((half - 1) * largest, TILE, LANES), BF16),
                pltpu.VMEM((tiles, TILE, LANES), BF16),
                pltpu.VMEM((len(merged), LANES), F32),
                pltpu.VMEM((half - 1, len(merged), LANES), F32),
                pltpu.VMEM((2, len(merged), LANES), F32),
                pltpu.VMEM((width, width), F32),
                pltpu.VMEM((width, width), BF16),
                pltpu.VMEM((n_entity, count, width), BF16),
                pltpu.VMEM((n_entity, count, width), BF16),
                pltpu.VMEM((1, n_entity * count), F32),
                pltpu.VMEM((n_entity, 1, n_entity * count), F32),
                pltpu.VMEM((n_entity * count, n_entity), F32),
                pltpu.SemaphoreType.DMA((LOADS + 1,)),
                pltpu.SemaphoreType.DMA((8,)),
                pltpu.SemaphoreType.DMA((8,)),
                pltpu.SemaphoreType.DMA,
                pltpu.SemaphoreType.DMA((half,)),
                pltpu.SemaphoreType.DMA((half,)),
                pltpu.SemaphoreType.DMA((half,)),
                pltpu.SemaphoreType.REGULAR,
            ],
            compiler_params=pltpu.CompilerParams(
                collective_id=0, has_side_effects=True, vmem_limit_bytes=48 << 20
            ),
            name="whiten_pool",
        )(*[pltpu.with_memory_space_constraint(a, pltpu.HBM) for a in (companies, queries)])

    return jax.shard_map(
        per_device,
        mesh=mesh,
        in_specs=(P("entity", None), P(("news", "entity"), None)),
        out_specs=P(("news", "entity"), None),
        check_vma=False,
    )
```

```python
import functools

import jax
import jax.numpy as jnp
from jax import lax
from jax.experimental import pallas as pl
from jax.experimental.pallas import tpu as pltpu
from jax.sharding import PartitionSpec as P

RIDGE = 0.05
EPSILON = 1e-06
MESH = pl.DeviceIdType.MESH
LANES = 128
LOADS = 2
TILE = 16
EVEN = 2
SLABS = 4
F32 = jnp.float32
BF16 = jnp.bfloat16


def dot(first_mat, second_mat):
    return jnp.dot(first_mat, second_mat, preferred_element_type=F32)


def upper_product(first_mat, second_mat):
    middle = first_mat.shape[0] // 2
    return (
        dot(first_mat[:middle, :], second_mat),
        dot(first_mat[middle:, :], second_mat[:, middle:]),
    )


def mirrored(parts):
    top, corner = (part.astype(BF16) for part in parts)
    middle = top.shape[0]
    bottom = jnp.concatenate([top[:, middle:].T, corner], axis=1)
    return jnp.concatenate([top, bottom], axis=0)


def add_unit(part, unit):
    rows = []
    for i in range(part.shape[0] // LANES):
        at = slice(i * LANES, (i + 1) * LANES)
        pieces = [part[at, : i * LANES], part[at, at] + unit, part[at, (i + 1) * LANES :]]
        rows.append(jnp.concatenate([piece for piece in pieces if piece.shape[1]], axis=1))
    return jnp.concatenate(rows, axis=0)


def remote(src_ref, dst_ref, sems, number, peer):
    send_sem, recv_sem = sems
    return pltpu.make_async_remote_copy(
        src_ref=src_ref,
        dst_ref=dst_ref,
        send_sem=send_sem.at[number],
        recv_sem=recv_sem.at[number],
        device_id={"entity": peer},
        device_id_type=MESH,
    )


def wait_bytes(ref, sem):
    pltpu.make_async_copy(ref, ref, sem).wait()


def flipped(chip, flip):
    bit, result = 1, chip
    while bit <= flip:
        if flip & bit:
            result = result + bit - 2 * bit * lax.rem(chip // bit, 2)
        bit *= 2
    return result


def core_shares(tiles, half):
    both = tiles // half
    first = max(1, both * EVEN // 8)
    return (0, first), (half * first, both - first)


def packing(n_blocks):
    merged = [(i, i) for i in range(0, n_blocks, 2)]
    return merged, [(i, j) for i in range(n_blocks) for j in range(i + 1, n_blocks)]


def kernel(
    n_entity,
    comp_hbm,
    query_hbm,
    out_ref,
    comp,
    query_all,
    gram_send,
    gram_pair,
    gram_recv,
    gram_all,
    diag_send,
    diag_recv,
    diag_sum,
    gram,
    gram_low,
    part_send,
    part_recv,
    tail_send,
    tail_recv,
    tail_cols,
    load_sem,
    send_sem,
    recv_sem,
    ring_send,
    ring_recv,
    pass_send,
    pass_recv,
    hello,
):
    rows, width = comp.shape
    count = query_hbm.shape[0]
    total_rows = rows * n_entity
    n_blocks = width // LANES
    per_block = LANES // TILE
    me = lax.axis_index("entity")
    half = n_entity // 2
    chip, core = me // 2, lax.rem(me, 2)
    sibling = me + 1 - 2 * core
    my_slot = core * half + chip
    sems = (send_sem, recv_sem)
    flips = list(range(half - 1, 0, -1))
    shares = core_shares(gram_send.shape[0], half)

    barrier = pltpu.get_barrier_semaphore()

    @pl.when(core == 1)
    def _():
        pl.semaphore_signal(
            barrier, inc=1, device_id={"entity": sibling}, device_id_type=MESH
        )

    load_chunks = LOADS
    chunk = rows // load_chunks
    loads = [
        pltpu.make_async_copy(
            comp_hbm.at[pl.ds(c * chunk, chunk)],
            comp.at[pl.ds(c * chunk, chunk)],
            load_sem.at[c],
        )
        for c in range(load_chunks)
    ]
    for load in loads:
        load.start()
    load_query = pltpu.make_async_copy(
        query_hbm, query_all.at[my_slot], load_sem.at[load_chunks]
    )
    load_query.start()

    @pl.when(core == 0)
    def _():
        pl.semaphore_wait(barrier, 1)
        pl.semaphore_signal(
            hello, inc=1, device_id={"entity": sibling}, device_id_type=MESH
        )

    @pl.when(core == 1)
    def _():
        pl.semaphore_wait(hello, 1)
        for flip in flips:
            pl.semaphore_signal(
                barrier,
                inc=1,
                device_id={"entity": 2 * flipped(chip, flip) + 1},
                device_id_type=MESH,
            )

    for load in loads:
        load.wait()
    merged, plain = packing(n_blocks)
    row_ids = lax.broadcasted_iota(jnp.int32, (LANES, LANES), 0)
    col_ids = lax.broadcasted_iota(jnp.int32, (LANES, LANES), 1)
    diagonals = {}
    items = merged + plain

    def pack(item, block):
        for t in range(per_block):
            gram_send[items.index(item) * per_block + t] = block[
                t * TILE : (t + 1) * TILE, :
            ].astype(BF16)

    for i in range(n_blocks):
        row_part = lax.dot_general(
            comp[:, i * LANES : (i + 1) * LANES],
            comp[:, i * LANES :],
            (((0,), (0,)), ((), ())),
            preferred_element_type=F32,
        )
        row_part = row_part * (1.0 / total_rows)
        diagonals[i] = row_part[:, :LANES]
        for j in range(i + 1, n_blocks):
            pack((i, j), row_part[:, (j - i) * LANES : (j - i + 1) * LANES])
        if i % 2:
            pack((i - 1, i - 1), jnp.where(row_ids <= col_ids, diagonals[i - 1], diagonals[i]))
            diag_send[i // 2 : i // 2 + 1, :] = jnp.sum(
                jnp.where(row_ids == col_ids, diagonals[i], 0.0), axis=0, keepdims=True
            )

    own_half = pl.ds(core * half, half)
    def to_pair(side):
        base, share = shares[1 - side]
        return pltpu.make_async_remote_copy(
            src_ref=gram_send.at[pl.ds(base, half * share)],
            dst_ref=gram_pair.at[pl.ds(0, half * share)],
            send_sem=send_sem.at[0],
            recv_sem=recv_sem.at[0],
            device_id={"entity": sibling},
            device_id_type=MESH,
        )

    def by_core(step):
        pl.when(core == 0)(functools.partial(step, 0))
        pl.when(core == 1)(functools.partial(step, 1))

    by_core(lambda side: to_pair(side).start())

    @pl.when(core == 1)
    def _():
        pl.semaphore_wait(barrier, half - 1)
        pl.semaphore_signal(
            hello, inc=1, device_id={"entity": sibling}, device_id_type=MESH
        )

    @pl.when(core == 0)
    def _():
        pl.semaphore_wait(hello, 1)

    load_query.wait()
    there = {flip: flipped(chip, flip) for flip in flips}

    def scatter(side):
        base, share = shares[side]
        to_pair(1 - side).wait_recv()
        gram_pair[: half * share] = (
            gram_pair[: half * share].astype(F32)
            + gram_send[base : base + half * share].astype(F32)
        ).astype(gram_pair.dtype)
        for q in range(half - 1):
            peer = q + (q >= chip).astype(jnp.int32)
            number = chip - (chip > peer).astype(jnp.int32)
            remote(
                gram_pair.at[pl.ds(peer * share, share)],
                gram_recv.at[pl.ds(number * share, share)],
                sems,
                1,
                2 * peer + core,
            ).start()

    by_core(scatter)
    for flip in flips:
        remote(
            query_all.at[my_slot], query_all.at[my_slot], sems, 2, 2 * there[flip] + core
        ).start()
    for flip in flips:
        remote(diag_send, diag_recv.at[flip - 1], sems, 3, 2 * there[flip] + core).start()

    def piece(side, owner):
        base, share = shares[side]
        return gram_all.at[pl.ds(base + owner * share, share)]

    def spread(side, owner, peer):
        return pltpu.make_async_remote_copy(
            src_ref=piece(side, owner),
            dst_ref=piece(side, owner),
            send_sem=ring_send,
            recv_sem=ring_recv.at[owner],
            device_id={"entity": 2 * peer + side},
            device_id_type=MESH,
        )

    def forward(side, number, owner):
        return pltpu.make_async_remote_copy(
            src_ref=piece(side, owner),
            dst_ref=piece(side, owner),
            send_sem=pass_send.at[number],
            recv_sem=pass_recv.at[number],
            device_id={"entity": sibling},
            device_id_type=MESH,
        )

    def gather(side):
        base, share = shares[side]
        arrived = gram_recv.at[pl.ds(0, (half - 1) * share)]
        wait_bytes(arrived, recv_sem.at[1])
        total = gram_pair[pl.ds(chip * share, share)].astype(F32)
        for k in range(half - 1):
            total = total + gram_recv[k * share : (k + 1) * share].astype(F32)
        gram_all[pl.ds(base + chip * share, share)] = total.astype(gram_all.dtype)
        for q in range(half - 1, 0, -1):
            peer = q - (q <= chip).astype(jnp.int32)
            spread(side, chip, peer).start()
        forward(side, 0, chip).start()

    by_core(gather)
    wait_bytes(diag_recv, recv_sem.at[3])
    diag_total = diag_send[...]
    for k in range(half - 1):
        diag_total = diag_total + diag_recv[k]
    diag_sum[0] = diag_total
    diag_forward = remote(diag_sum.at[0], diag_sum.at[1], sems, 4, sibling)
    diag_forward.start()
    arrivals = sorted(flips, key=lambda flip: (bin(flip).count("1") + flip // 4, flip))

    def pass_on(side):
        for flip in arrivals:
            spread(side, there[flip], there[flip]).wait_recv()
            forward(side, flip, there[flip]).start()

    by_core(pass_on)
    wait_bytes(query_all.at[pl.ds(0, half - 1)], recv_sem.at[2])
    query_forward = remote(query_all.at[own_half], query_all.at[own_half], sems, 5, sibling)
    query_forward.start()
    diag_forward.wait_recv()

    ridge = jnp.where(row_ids == col_ids, RIDGE, 0.0)
    diag_rows = diag_sum[0] + diag_sum[1]

    def place(i, j, value):
        at = (slice(i * LANES, (i + 1) * LANES), slice(j * LANES, (j + 1) * LANES))
        if i < n_blocks // 2 or j >= n_blocks // 2:
            gram[at] = value
        gram_low[at] = value.astype(BF16)

    def unpack(whose):
        for number, (i, j) in enumerate(items):
            if owner_of(number) != whose:
                continue
            block = (
                gram_all[number * per_block : (number + 1) * per_block]
                .astype(F32)
                .reshape(LANES, LANES)
            )
            turned = block.T
            if i != j:
                place(i, j, block)
                place(j, i, turned)
            else:
                even = jnp.where(row_ids <= col_ids, block, turned) + ridge
                odd = jnp.where(row_ids > col_ids, block, turned)
                odd = jnp.where(row_ids == col_ids, diag_rows[i // 2 : i // 2 + 1, :], odd)
                place(i, i, even)
                place(i + 1, i + 1, odd + ridge)

    def owner_of(number):
        return int(number * per_block >= shares[1][0])

    by_core(unpack)
    def passed(side):
        for flip in [0] + arrivals:
            forward(1 - side, flip, chip).wait_recv()

    by_core(passed)
    by_core(lambda side: unpack(1 - side))
    squares = jnp.zeros((LANES, LANES), F32)
    for i in range(n_blocks):
        for j in range(i, n_blocks):
            block = gram[i * LANES : (i + 1) * LANES, j * LANES : (j + 1) * LANES]
            squares = squares + (1.0 if i == j else 2.0) * (block * block)
    squares = jnp.sum(squares, axis=0, keepdims=True)
    frob_square = jnp.sum(squares, axis=1, keepdims=True) + EPSILON
    frob_norm = jnp.sqrt(frob_square)
    inverse = 1.0 / frob_norm
    inverse_square = inverse * inverse
    root = 1.0 / jnp.sqrt(frob_norm)
    middle = width // 2
    low = gram_low[...]
    full = (gram[:middle, :], gram[middle:, middle:])
    second = upper_product(low, low)
    inner = mirrored([a - (4.5 * frob_norm) * b for a, b in zip(second, full)])
    fourth = upper_product(inner, inner)
    z_rest = [
        (0.421875 * inverse_square) * a
        - (2.4375 * inverse) * b
        + (0.0625 * inverse_square * inverse_square) * c
        for a, b, c in zip(second, full, fourth)
    ]
    z_low = mirrored(z_rest)
    y_two = [2.25 * a + b for a, b in zip(full, upper_product(low, z_low))]
    y_low = mirrored(y_two)
    q_low = mirrored([4.5 * a + b for a, b in zip(z_rest, upper_product(z_low, z_low))])
    last = upper_product(y_low, q_low)
    z_three = [
        (1.5 * root) * a - (inverse * root) * (2.53125 * b + 0.5 * c)
        for a, b, c in zip(z_rest, y_two, last)
    ]
    unit = jnp.where(row_ids == col_ids, 3.375 * root, 0.0)
    whitener = mirrored([add_unit(part, unit) for part in z_three])

    query_forward.wait_recv()
    query_block = query_all[...].astype(F32).reshape(n_entity * count, width).astype(BF16)
    white_query = dot(query_block, whitener).astype(BF16)
    score_scale = width ** (-0.5)
    slab_chunk = rows // SLABS
    slabs = [
        dot(comp[c * slab_chunk : (c + 1) * slab_chunk, :], whitener).astype(BF16)
        for c in range(SLABS)
    ]
    scores = [
        lax.dot_general(
            white_query, slab, (((1,), (1,)), ((), ())), preferred_element_type=F32
        )
        for slab in slabs
    ]
    tops = [jnp.max(part, axis=1, keepdims=True) for part in scores]
    weights = [jnp.exp((part - top) * score_scale) for part, top in zip(scores, tops)]
    denoms = [jnp.sum(part, axis=1, keepdims=True) for part in weights]
    sums = [dot(part.astype(BF16), slab) for part, slab in zip(weights, slabs)]
    top = functools.reduce(jnp.maximum, tops)
    scales = [jnp.exp((part - top) * score_scale) for part in tops]
    denom = functools.reduce(jnp.add, [a * b for a, b in zip(scales, denoms)])
    level = top * score_scale + jnp.log(denom)
    level_row = jnp.broadcast_to(level, (n_entity * count, LANES)).T[0:1, :]
    tail_send[...] = level_row
    tail_recv[my_slot] = level_row
    for k in range(n_entity - 1):
        peer = k + (k >= me).astype(jnp.int32)
        remote(tail_send, tail_recv.at[my_slot], sems, 7, peer).start()
    share = 1.0 / denom
    summed = functools.reduce(jnp.add, [(a * share) * b for a, b in zip(scales, sums)])
    for k in range(n_entity):
        part_send[k] = summed[k * count : (k + 1) * count, :].astype(BF16)
    for k in range(n_entity - 1):
        peer = k + (k >= me).astype(jnp.int32)
        peer_slot = lax.rem(peer, 2) * half + peer // 2
        remote(part_send.at[peer_slot], part_recv.at[my_slot], sems, 6, peer).start()
    def sent(side):
        share = shares[side][1]
        to_pair(side).wait_send()
        wait_bytes(gram_recv.at[pl.ds(0, (half - 1) * share)], send_sem.at[1])
        for _ in range(half - 1):
            spread(side, chip, chip).wait_send()
        for flip in [0] + arrivals:
            forward(side, flip, chip).wait_send()

    by_core(sent)
    wait_bytes(query_all.at[pl.ds(0, half - 1)], send_sem.at[2])
    wait_bytes(diag_recv, send_sem.at[3])
    diag_forward.wait_send()
    query_forward.wait_send()
    wait_bytes(part_recv.at[pl.ds(0, n_entity - 1)], send_sem.at[6])
    wait_bytes(tail_recv.at[pl.ds(0, n_entity - 1)], send_sem.at[7])
    wait_bytes(tail_recv.at[pl.ds(0, n_entity - 1)], recv_sem.at[7])
    levels = tail_recv[...].reshape(n_entity, n_entity * count)
    tail_cols[...] = levels.T
    mine = tail_cols[pl.ds(pl.multiple_of(my_slot * count, count), count), :]
    factors = jnp.exp(mine - jnp.max(mine, axis=1, keepdims=True))
    factors = factors * (1.0 / jnp.sum(factors, axis=1, keepdims=True))
    wait_bytes(part_recv.at[pl.ds(0, n_entity - 1)], recv_sem.at[6])
    part_recv[my_slot] = part_send[my_slot]
    parts = [part_recv[k] for k in range(n_entity)]
    out_ref[...] = functools.reduce(
        jnp.add, [factors[:, k : k + 1] * part.astype(F32) for k, part in enumerate(parts)]
    )


def solution(mesh):
    n_entity = mesh.shape["entity"]

    def per_device(companies, queries):
        rows, width = companies.shape
        count = queries.shape[0]
        half = n_entity // 2
        merged, plain = packing(width // LANES)
        tiles = (len(merged) + len(plain)) * LANES // TILE
        largest = max(share for _, share in core_shares(tiles, half))
        return pl.pallas_call(
            functools.partial(kernel, n_entity),
            out_shape=jax.ShapeDtypeStruct((count, width), F32),
            in_specs=[
                pl.BlockSpec(memory_space=pltpu.HBM),
                pl.BlockSpec(memory_space=pltpu.HBM),
            ],
            out_specs=pl.BlockSpec(memory_space=pltpu.VMEM),
            scratch_shapes=[
                pltpu.VMEM((rows, width), BF16),
                pltpu.VMEM((n_entity, count, width), BF16),
                pltpu.VMEM((tiles, TILE, LANES), BF16),
                pltpu.VMEM((half * largest, TILE, LANES), BF16),
                pltpu.VMEM(((half - 1) * largest, TILE, LANES), BF16),
                pltpu.VMEM((tiles, TILE, LANES), BF16),
                pltpu.VMEM((len(merged), LANES), F32),
                pltpu.VMEM((half - 1, len(merged), LANES), F32),
                pltpu.VMEM((2, len(merged), LANES), F32),
                pltpu.VMEM((width, width), F32),
                pltpu.VMEM((width, width), BF16),
                pltpu.VMEM((n_entity, count, width), BF16),
                pltpu.VMEM((n_entity, count, width), BF16),
                pltpu.VMEM((1, n_entity * count), F32),
                pltpu.VMEM((n_entity, 1, n_entity * count), F32),
                pltpu.VMEM((n_entity * count, n_entity), F32),
                pltpu.SemaphoreType.DMA((LOADS + 1,)),
                pltpu.SemaphoreType.DMA((8,)),
                pltpu.SemaphoreType.DMA((8,)),
                pltpu.SemaphoreType.DMA,
                pltpu.SemaphoreType.DMA((half,)),
                pltpu.SemaphoreType.DMA((half,)),
                pltpu.SemaphoreType.DMA((half,)),
                pltpu.SemaphoreType.REGULAR,
            ],
            compiler_params=pltpu.CompilerParams(
                collective_id=0, has_side_effects=True, vmem_limit_bytes=48 << 20
            ),
            name="whiten_pool",
        )(*[pltpu.with_memory_space_constraint(a, pltpu.HBM) for a in (companies, queries)])

    return jax.shard_map(
        per_device,
        mesh=mesh,
        in_specs=(P("entity", None), P(("news", "entity"), None)),
        out_specs=P(("news", "entity"), None),
        check_vma=False,
    )
```

```python
import functools

import jax
import jax.numpy as jnp
from jax import lax
from jax.experimental import pallas as pl
from jax.experimental.pallas import tpu as pltpu
from jax.sharding import PartitionSpec as P

RIDGE = 0.05
EPSILON = 1e-06
MESH = pl.DeviceIdType.MESH
LANES = 128
LOADS = 2
TILE = 16
EVEN = 2
SLABS = 2
F32 = jnp.float32
BF16 = jnp.bfloat16


def dot(first_mat, second_mat):
    return jnp.dot(first_mat, second_mat, preferred_element_type=F32)


def upper_product(first_mat, second_mat):
    middle = first_mat.shape[0] // 2
    return (
        dot(first_mat[:middle, :], second_mat),
        dot(first_mat[middle:, :], second_mat[:, middle:]),
    )


def mirrored(parts):
    top, corner = (part.astype(BF16) for part in parts)
    middle = top.shape[0]
    bottom = jnp.concatenate([top[:, middle:].T, corner], axis=1)
    return jnp.concatenate([top, bottom], axis=0)


def add_unit(part, unit):
    rows = []
    for i in range(part.shape[0] // LANES):
        at = slice(i * LANES, (i + 1) * LANES)
        pieces = [part[at, : i * LANES], part[at, at] + unit, part[at, (i + 1) * LANES :]]
        rows.append(jnp.concatenate([piece for piece in pieces if piece.shape[1]], axis=1))
    return jnp.concatenate(rows, axis=0)


def remote(src_ref, dst_ref, sems, number, peer):
    send_sem, recv_sem = sems
    return pltpu.make_async_remote_copy(
        src_ref=src_ref,
        dst_ref=dst_ref,
        send_sem=send_sem.at[number],
        recv_sem=recv_sem.at[number],
        device_id={"entity": peer},
        device_id_type=MESH,
    )


def wait_bytes(ref, sem):
    pltpu.make_async_copy(ref, ref, sem).wait()


def flipped(chip, flip):
    bit, result = 1, chip
    while bit <= flip:
        if flip & bit:
            result = result + bit - 2 * bit * lax.rem(chip // bit, 2)
        bit *= 2
    return result


def core_shares(tiles, half):
    both = tiles // half
    first = max(1, both * EVEN // 8)
    return (0, first), (half * first, both - first)


def packing(n_blocks):
    merged = [(i, i) for i in range(0, n_blocks, 2)]
    return merged, [(i, j) for i in range(n_blocks) for j in range(i + 1, n_blocks)]


def kernel(
    n_entity,
    comp_hbm,
    query_hbm,
    out_ref,
    comp,
    query_all,
    gram_send,
    gram_pair,
    gram_recv,
    gram_all,
    diag_send,
    diag_recv,
    diag_sum,
    gram,
    gram_low,
    part_send,
    part_recv,
    tail_send,
    tail_recv,
    tail_cols,
    load_sem,
    send_sem,
    recv_sem,
    ring_send,
    ring_recv,
    pass_send,
    pass_recv,
    hello,
):
    rows, width = comp.shape
    count = query_hbm.shape[0]
    total_rows = rows * n_entity
    n_blocks = width // LANES
    per_block = LANES // TILE
    me = lax.axis_index("entity")
    half = n_entity // 2
    chip, core = me // 2, lax.rem(me, 2)
    sibling = me + 1 - 2 * core
    my_slot = core * half + chip
    sems = (send_sem, recv_sem)
    flips = list(range(half - 1, 0, -1))
    shares = core_shares(gram_send.shape[0], half)

    barrier = pltpu.get_barrier_semaphore()

    @pl.when(core == 1)
    def _():
        pl.semaphore_signal(
            barrier, inc=1, device_id={"entity": sibling}, device_id_type=MESH
        )

    load_chunks = LOADS
    chunk = rows // load_chunks
    loads = [
        pltpu.make_async_copy(
            comp_hbm.at[pl.ds(c * chunk, chunk)],
            comp.at[pl.ds(c * chunk, chunk)],
            load_sem.at[c],
        )
        for c in range(load_chunks)
    ]
    for load in loads:
        load.start()
    load_query = pltpu.make_async_copy(
        query_hbm, query_all.at[my_slot], load_sem.at[load_chunks]
    )
    load_query.start()

    @pl.when(core == 0)
    def _():
        pl.semaphore_wait(barrier, 1)
        pl.semaphore_signal(
            hello, inc=1, device_id={"entity": sibling}, device_id_type=MESH
        )

    @pl.when(core == 1)
    def _():
        pl.semaphore_wait(hello, 1)
        for flip in flips:
            pl.semaphore_signal(
                barrier,
                inc=1,
                device_id={"entity": 2 * flipped(chip, flip) + 1},
                device_id_type=MESH,
            )

    for load in loads:
        load.wait()
    merged, plain = packing(n_blocks)
    row_ids = lax.broadcasted_iota(jnp.int32, (LANES, LANES), 0)
    col_ids = lax.broadcasted_iota(jnp.int32, (LANES, LANES), 1)
    diagonals = {}
    items = merged + plain

    def pack(item, block):
        for t in range(per_block):
            gram_send[items.index(item) * per_block + t] = block[
                t * TILE : (t + 1) * TILE, :
            ].astype(BF16)

    for i in range(n_blocks):
        row_part = lax.dot_general(
            comp[:, i * LANES : (i + 1) * LANES],
            comp[:, i * LANES :],
            (((0,), (0,)), ((), ())),
            preferred_element_type=F32,
        )
        row_part = row_part * (1.0 / total_rows)
        diagonals[i] = row_part[:, :LANES]
        for j in range(i + 1, n_blocks):
            pack((i, j), row_part[:, (j - i) * LANES : (j - i + 1) * LANES])
        if i % 2:
            pack((i - 1, i - 1), jnp.where(row_ids <= col_ids, diagonals[i - 1], diagonals[i]))
            diag_send[i // 2 : i // 2 + 1, :] = jnp.sum(
                jnp.where(row_ids == col_ids, diagonals[i], 0.0), axis=0, keepdims=True
            )

    own_half = pl.ds(core * half, half)
    def to_pair(side):
        base, share = shares[1 - side]
        return pltpu.make_async_remote_copy(
            src_ref=gram_send.at[pl.ds(base, half * share)],
            dst_ref=gram_pair.at[pl.ds(0, half * share)],
            send_sem=send_sem.at[0],
            recv_sem=recv_sem.at[0],
            device_id={"entity": sibling},
            device_id_type=MESH,
        )

    def by_core(step):
        pl.when(core == 0)(functools.partial(step, 0))
        pl.when(core == 1)(functools.partial(step, 1))

    by_core(lambda side: to_pair(side).start())

    @pl.when(core == 1)
    def _():
        pl.semaphore_wait(barrier, half - 1)
        pl.semaphore_signal(
            hello, inc=1, device_id={"entity": sibling}, device_id_type=MESH
        )

    @pl.when(core == 0)
    def _():
        pl.semaphore_wait(hello, 1)

    load_query.wait()
    there = {flip: flipped(chip, flip) for flip in flips}

    def scatter(side):
        base, share = shares[side]
        to_pair(1 - side).wait_recv()
        gram_pair[: half * share] = (
            gram_pair[: half * share].astype(F32)
            + gram_send[base : base + half * share].astype(F32)
        ).astype(gram_pair.dtype)
        for q in range(half - 1):
            peer = q + (q >= chip).astype(jnp.int32)
            number = chip - (chip > peer).astype(jnp.int32)
            remote(
                gram_pair.at[pl.ds(peer * share, share)],
                gram_recv.at[pl.ds(number * share, share)],
                sems,
                1,
                2 * peer + core,
            ).start()

    by_core(scatter)
    for flip in flips:
        remote(
            query_all.at[my_slot], query_all.at[my_slot], sems, 2, 2 * there[flip] + core
        ).start()
    for flip in flips:
        remote(diag_send, diag_recv.at[flip - 1], sems, 3, 2 * there[flip] + core).start()

    def piece(side, owner):
        base, share = shares[side]
        return gram_all.at[pl.ds(base + owner * share, share)]

    def spread(side, owner, peer):
        return pltpu.make_async_remote_copy(
            src_ref=piece(side, owner),
            dst_ref=piece(side, owner),
            send_sem=ring_send,
            recv_sem=ring_recv.at[owner],
            device_id={"entity": 2 * peer + side},
            device_id_type=MESH,
        )

    def forward(side, number, owner):
        return pltpu.make_async_remote_copy(
            src_ref=piece(side, owner),
            dst_ref=piece(side, owner),
            send_sem=pass_send.at[number],
            recv_sem=pass_recv.at[number],
            device_id={"entity": sibling},
            device_id_type=MESH,
        )

    def gather(side):
        base, share = shares[side]
        arrived = gram_recv.at[pl.ds(0, (half - 1) * share)]
        wait_bytes(arrived, recv_sem.at[1])
        total = gram_pair[pl.ds(chip * share, share)].astype(F32)
        for k in range(half - 1):
            total = total + gram_recv[k * share : (k + 1) * share].astype(F32)
        gram_all[pl.ds(base + chip * share, share)] = total.astype(gram_all.dtype)
        for q in range(half - 1, 0, -1):
            peer = q - (q <= chip).astype(jnp.int32)
            spread(side, chip, peer).start()
        forward(side, 0, chip).start()

    by_core(gather)
    wait_bytes(diag_recv, recv_sem.at[3])
    diag_total = diag_send[...]
    for k in range(half - 1):
        diag_total = diag_total + diag_recv[k]
    diag_sum[0] = diag_total
    diag_forward = remote(diag_sum.at[0], diag_sum.at[1], sems, 4, sibling)
    diag_forward.start()
    arrivals = sorted(flips, key=lambda flip: (bin(flip).count("1") + flip // 4, flip))

    def pass_on(side):
        for flip in arrivals:
            spread(side, there[flip], there[flip]).wait_recv()
            forward(side, flip, there[flip]).start()

    by_core(pass_on)
    wait_bytes(query_all.at[pl.ds(0, half - 1)], recv_sem.at[2])
    query_forward = remote(query_all.at[own_half], query_all.at[own_half], sems, 5, sibling)
    query_forward.start()
    diag_forward.wait_recv()

    def passed(side):
        for flip in [0] + arrivals:
            forward(1 - side, flip, chip).wait_recv()

    by_core(passed)
    diag_rows = diag_sum[0] + diag_sum[1]

    ridge = jnp.where(row_ids == col_ids, RIDGE, 0.0)
    squares = jnp.zeros((LANES, LANES), F32)

    def place(i, j, value):
        at = (slice(i * LANES, (i + 1) * LANES), slice(j * LANES, (j + 1) * LANES))
        if i < n_blocks // 2 or j >= n_blocks // 2:
            gram[at] = value
        gram_low[at] = value.astype(BF16)

    for number, (i, j) in enumerate(items):
        block = (
            gram_all[number * per_block : (number + 1) * per_block]
            .astype(F32)
            .reshape(LANES, LANES)
        )
        turned = block.T
        if i != j:
            place(i, j, block)
            place(j, i, turned)
            squares = squares + 2.0 * (block * block)
        else:
            even = jnp.where(row_ids <= col_ids, block, turned) + ridge
            odd = jnp.where(row_ids > col_ids, block, turned)
            odd = jnp.where(row_ids == col_ids, diag_rows[i // 2 : i // 2 + 1, :], odd) + ridge
            place(i, i, even)
            place(i + 1, i + 1, odd)
            squares = squares + even * even + odd * odd

    squares = jnp.sum(squares, axis=0, keepdims=True)
    frob_square = jnp.sum(squares, axis=1, keepdims=True) + EPSILON
    frob_norm = jnp.sqrt(frob_square)
    inverse = 1.0 / frob_norm
    inverse_square = inverse * inverse
    root = 1.0 / jnp.sqrt(frob_norm)
    middle = width // 2
    low = gram_low[...]
    full = (gram[:middle, :], gram[middle:, middle:])
    second = upper_product(low, low)
    inner = mirrored([a - (4.5 * frob_norm) * b for a, b in zip(second, full)])
    fourth = upper_product(inner, inner)
    z_rest = [
        (0.421875 * inverse_square) * a
        - (2.4375 * inverse) * b
        + (0.0625 * inverse_square * inverse_square) * c
        for a, b, c in zip(second, full, fourth)
    ]
    z_low = mirrored(z_rest)
    y_two = [2.25 * a + b for a, b in zip(full, upper_product(low, z_low))]
    y_low = mirrored(y_two)
    q_low = mirrored([4.5 * a + b for a, b in zip(z_rest, upper_product(z_low, z_low))])
    last = upper_product(y_low, q_low)
    z_three = [
        (1.5 * root) * a - (inverse * root) * (2.53125 * b + 0.5 * c)
        for a, b, c in zip(z_rest, y_two, last)
    ]
    unit = jnp.where(row_ids == col_ids, 3.375 * root, 0.0)
    whitener = mirrored([add_unit(part, unit) for part in z_three])

    query_forward.wait_recv()
    query_block = query_all[...].astype(F32).reshape(n_entity * count, width).astype(BF16)
    white_query = dot(query_block, whitener).astype(BF16)
    score_scale = width ** (-0.5)
    slab_chunk = rows // SLABS
    slabs = [
        dot(comp[c * slab_chunk : (c + 1) * slab_chunk, :], whitener).astype(BF16)
        for c in range(SLABS)
    ]
    scores = [
        lax.dot_general(
            white_query, slab, (((1,), (1,)), ((), ())), preferred_element_type=F32
        )
        for slab in slabs
    ]
    tops = [jnp.max(part, axis=1, keepdims=True) for part in scores]
    weights = [jnp.exp((part - top) * score_scale) for part, top in zip(scores, tops)]
    denoms = [jnp.sum(part, axis=1, keepdims=True) for part in weights]
    sums = [dot(part.astype(BF16), slab) for part, slab in zip(weights, slabs)]
    top = functools.reduce(jnp.maximum, tops)
    scales = [jnp.exp((part - top) * score_scale) for part in tops]
    denom = functools.reduce(jnp.add, [a * b for a, b in zip(scales, denoms)])
    level = top * score_scale + jnp.log(denom)
    level_row = jnp.broadcast_to(level, (n_entity * count, LANES)).T[0:1, :]
    tail_send[...] = level_row
    tail_recv[my_slot] = level_row
    for k in range(n_entity - 1):
        peer = k + (k >= me).astype(jnp.int32)
        remote(tail_send, tail_recv.at[my_slot], sems, 7, peer).start()
    share = 1.0 / denom
    summed = functools.reduce(jnp.add, [(a * share) * b for a, b in zip(scales, sums)])
    for k in range(n_entity):
        part_send[k] = summed[k * count : (k + 1) * count, :].astype(BF16)
    for k in range(n_entity - 1):
        peer = k + (k >= me).astype(jnp.int32)
        peer_slot = lax.rem(peer, 2) * half + peer // 2
        remote(part_send.at[peer_slot], part_recv.at[my_slot], sems, 6, peer).start()
    def sent(side):
        share = shares[side][1]
        to_pair(side).wait_send()
        wait_bytes(gram_recv.at[pl.ds(0, (half - 1) * share)], send_sem.at[1])
        for _ in range(half - 1):
            spread(side, chip, chip).wait_send()
        for flip in [0] + arrivals:
            forward(side, flip, chip).wait_send()

    by_core(sent)
    wait_bytes(query_all.at[pl.ds(0, half - 1)], send_sem.at[2])
    wait_bytes(diag_recv, send_sem.at[3])
    diag_forward.wait_send()
    query_forward.wait_send()
    wait_bytes(part_recv.at[pl.ds(0, n_entity - 1)], send_sem.at[6])
    wait_bytes(tail_recv.at[pl.ds(0, n_entity - 1)], send_sem.at[7])
    wait_bytes(tail_recv.at[pl.ds(0, n_entity - 1)], recv_sem.at[7])
    levels = tail_recv[...].reshape(n_entity, n_entity * count)
    tail_cols[...] = levels.T
    mine = tail_cols[pl.ds(pl.multiple_of(my_slot * count, count), count), :]
    factors = jnp.exp(mine - jnp.max(mine, axis=1, keepdims=True))
    factors = factors * (1.0 / jnp.sum(factors, axis=1, keepdims=True))
    wait_bytes(part_recv.at[pl.ds(0, n_entity - 1)], recv_sem.at[6])
    part_recv[my_slot] = part_send[my_slot]
    parts = [part_recv[k] for k in range(n_entity)]
    out_ref[...] = functools.reduce(
        jnp.add, [factors[:, k : k + 1] * part.astype(F32) for k, part in enumerate(parts)]
    )


def solution(mesh):
    n_entity = mesh.shape["entity"]

    def per_device(companies, queries):
        rows, width = companies.shape
        count = queries.shape[0]
        half = n_entity // 2
        merged, plain = packing(width // LANES)
        tiles = (len(merged) + len(plain)) * LANES // TILE
        largest = max(share for _, share in core_shares(tiles, half))
        return pl.pallas_call(
            functools.partial(kernel, n_entity),
            out_shape=jax.ShapeDtypeStruct((count, width), F32),
            in_specs=[
                pl.BlockSpec(memory_space=pltpu.HBM),
                pl.BlockSpec(memory_space=pltpu.HBM),
            ],
            out_specs=pl.BlockSpec(memory_space=pltpu.VMEM),
            scratch_shapes=[
                pltpu.VMEM((rows, width), BF16),
                pltpu.VMEM((n_entity, count, width), BF16),
                pltpu.VMEM((tiles, TILE, LANES), BF16),
                pltpu.VMEM((half * largest, TILE, LANES), BF16),
                pltpu.VMEM(((half - 1) * largest, TILE, LANES), BF16),
                pltpu.VMEM((tiles, TILE, LANES), BF16),
                pltpu.VMEM((len(merged), LANES), F32),
                pltpu.VMEM((half - 1, len(merged), LANES), F32),
                pltpu.VMEM((2, len(merged), LANES), F32),
                pltpu.VMEM((width, width), F32),
                pltpu.VMEM((width, width), BF16),
                pltpu.VMEM((n_entity, count, width), BF16),
                pltpu.VMEM((n_entity, count, width), BF16),
                pltpu.VMEM((1, n_entity * count), F32),
                pltpu.VMEM((n_entity, 1, n_entity * count), F32),
                pltpu.VMEM((n_entity * count, n_entity), F32),
                pltpu.SemaphoreType.DMA((LOADS + 1,)),
                pltpu.SemaphoreType.DMA((8,)),
                pltpu.SemaphoreType.DMA((8,)),
                pltpu.SemaphoreType.DMA,
                pltpu.SemaphoreType.DMA((half,)),
                pltpu.SemaphoreType.DMA((half,)),
                pltpu.SemaphoreType.DMA((half,)),
                pltpu.SemaphoreType.REGULAR,
            ],
            compiler_params=pltpu.CompilerParams(
                collective_id=0, has_side_effects=True, vmem_limit_bytes=48 << 20
            ),
            name="whiten_pool",
        )(*[pltpu.with_memory_space_constraint(a, pltpu.HBM) for a in (companies, queries)])

    return jax.shard_map(
        per_device,
        mesh=mesh,
        in_specs=(P("entity", None), P(("news", "entity"), None)),
        out_specs=P(("news", "entity"), None),
        check_vma=False,
    )
```
